32 devices in a mesh: dp: 8 (over z, x), seq: 4 (over y, core).
Axes of the slice: x: 2, y: 2, z: 4, core: 2. Of those that a mesh axis runs over, the one named last changes fastest.
Arguments:
- tokens: bfloat16 [8, 1024, 1600], P('dp', 'seq'), may hold values from -6 to 6
- cotangent: bfloat16 [8, 1024, 1600], P('dp', 'seq'), may hold values from -6 to 6
- lengths: int32 [8], P('dp'), may hold values from 256 to 1024, as said below
- w_qkv: bfloat16 [7680000], P(('dp', 'seq')), may hold values from -0.15625 to 0.15625
- w_out: bfloat16 [2560000], P(('dp', 'seq')), may hold values from -2.5 to 2.5
- w_fc: bfloat16 [10246400], P(('dp', 'seq')), may hold values from -0.15625 to 0.15625
- w_proj: bfloat16 [10240000], P(('dp', 'seq')), may hold values from -0.078125 to 0.078125
- attention_vectors: bfloat16 [6400], P(('dp', 'seq')), as said below
- block_vectors: bfloat16 [6400], P(('dp', 'seq')), as said below
Outputs:
- output: bfloat16 [8, 1024, 1600], P('dp', 'seq')
- input_grad: float32 [8, 1024, 1600], P('dp', 'seq')
- grad_qkv: float32 [7680000], P(('dp', 'seq'))
- grad_out: float32 [2560000], P(('dp', 'seq'))
- grad_fc: float32 [10246400], P(('dp', 'seq'))
- grad_proj: float32 [10240000], P(('dp', 'seq'))
- grad_attention_vectors: float32 [6400], P(('dp', 'seq'))
- grad_block_vectors: float32 [6400], P(('dp', 'seq'))
The draws below stay inside these ranges and needn't reach their ends.
Inputs may be any that keep to these rules, and one draw needn't show every extreme that they name: `lengths`: valid positions of each slot; in every draw one slot has all 1024 and one has 256. `attention_vectors`: gains near one, biases of order one half. `block_vectors`: gains near one, biases of order one half.
All inputs are finite; a program needn't handle non-finite values.
Results may differ from the reference program's by a relative error of at most 0.01.
Values may be sent and summed in bfloat16 or wider, within the bound.
No kernel may reach another device: no remote copies, remote signals or barrier semaphores. Data moves between devices by JAX's collectives and lax.ppermute only.
A program may use at most 448 MiB of HBM per device.

```python
import math
import jax
import jax.numpy as jnp
from jax import lax

D = 1600
H = 25
HD = 64
FF = 6400
LENGTH = 1024
SLOTS = 8


def draw_tokens(key, part):
    offset = jax.random.normal(jax.random.fold_in(key, 31), (D,), jnp.float32)
    noise = jax.random.normal(jax.random.fold_in(key, 32), (SLOTS, LENGTH, D), jnp.float32)
    value = jnp.clip(0.8 * noise + 0.7 * offset, -6.0, 6.0)
    return value.astype(jnp.bfloat16)


def draw_lengths(key, part):
    base = jax.random.randint(jax.random.fold_in(key, 11), (SLOTS,), LENGTH // 4, LENGTH + 1)
    order = jax.random.permutation(jax.random.fold_in(key, 12), SLOTS)
    base = base.at[order[0]].set(LENGTH)
    base = base.at[order[1]].set(LENGTH // 4)
    return base.astype(jnp.int32)


def vector_noise(key, total):
    return jax.random.normal(key, (total,), jnp.float32)


def draw_attention_vectors(key, part):
    total = 4 * D
    which = jnp.arange(total) // D
    noise = vector_noise(jax.random.fold_in(key, 21), total)
    value = jnp.where(which == 0, 1.0 + 0.25 * noise, 0.5 * noise)
    return value.astype(jnp.bfloat16)


def draw_block_vectors(key, part):
    total = 4 * D
    which = jnp.arange(total) // D
    noise = vector_noise(jax.random.fold_in(key, 22), total)
    value = jnp.where(which == 1, 1.0 + 0.25 * noise, 0.5 * noise)
    return value.astype(jnp.bfloat16)


def levels(key, extent, pieces, smallest, top_value):
    loudness, own = 1.0, jax.random.fold_in(key, 6)
    for position, blocks in pieces:
        steps = jnp.exp(jax.random.uniform(jax.random.fold_in(own, position), (blocks,), jnp.float32, smallest / len(pieces), top_value / len(pieces)))
        loudness = loudness * jnp.repeat(steps, extent[position] // blocks).reshape([-1 if axis == position else 1 for axis in range(len(extent))])
    return loudness


def centred(own_key, dims, scale, reach, shards=(), kind=jnp.bfloat16):
    factor_of = levels(own_key, dims, shards, -0.22, 0.18) if shards else 1.0
    drawn = jax.random.normal(own_key, dims, jnp.float32) * scale * factor_of
    return jnp.minimum(jnp.maximum(drawn, -reach), reach).astype(kind)


def setup_inputs(seed: int = 0) -> dict:
    streams_of = jax.random.split(jax.random.key(seed), 10)
    tokens = draw_tokens(jax.random.fold_in(streams_of[9], 71), 0)
    cotangent = centred(streams_of[1], (SLOTS, LENGTH, D), 1.0, 6.0, ((0, 8), (1, 4)))
    lengths = draw_lengths(jax.random.fold_in(streams_of[9], 71), 0)
    w_qkv = centred(streams_of[3], (3 * D * D,), D ** -0.5, 0.15625, ((0, 32),))
    w_out = centred(streams_of[4], (D * D,), (max(D // 256, 1)) ** -0.5, 2.5, ((0, 32),))
    w_fc = centred(streams_of[5], ((D + 1) * FF,), D ** -0.5, 0.15625, ((0, 32),))
    w_proj = centred(streams_of[6], (FF * D,), FF ** -0.5, 0.078125, ((0, 32),))
    attention_vectors = draw_attention_vectors(jax.random.fold_in(streams_of[9], 71), 0)
    block_vectors = draw_block_vectors(jax.random.fold_in(streams_of[9], 71), 0)
    return dict(tokens=tokens, cotangent=cotangent, lengths=lengths, w_qkv=w_qkv, w_out=w_out, w_fc=w_fc, w_proj=w_proj, attention_vectors=attention_vectors, block_vectors=block_vectors)


@jax.custom_vjp
def low(v):
    return lax.optimization_barrier(v.astype(jnp.bfloat16)).astype(jnp.float32)

@jax.custom_vjp
def low_back(v):
    return v

def low_keep(v):
    return (low(v), None)

def low_pass(kept, grad):
    return (grad,)

def back_keep(v):
    return (v, None)

def back_low(kept, grad):
    return (low(grad),)
low.defvjp(low_keep, low_pass)
low_back.defvjp(back_keep, back_low)
EPS = 1e-05
HIGH_PRECISION = lax.Precision.HIGHEST

def layer_norm(value, gain, shift):
    centre = value - lax.optimization_barrier(jnp.mean(value, axis=-1, keepdims=True))
    spread = lax.optimization_barrier(jnp.mean(centre * centre, axis=-1, keepdims=True))
    return centre * lax.rsqrt(spread + EPS) * gain + shift

def tanh_gelu(value):
    return jax.nn.gelu(value, approximate=True)

def attend_slot(query, key_rows, value_rows, length):
    raw = jnp.einsum('qhd,khd->hqk', query, key_rows, precision=HIGH_PRECISION)
    scores = low_back(raw) * 0.125
    place = jnp.arange(LENGTH)
    allowed = (place[None, :] <= place[:, None]) & (place[None, :] < length)
    scores = jnp.where(allowed[None], scores, -1e+30)
    weights = low(jax.nn.softmax(scores, axis=-1))
    return jnp.einsum('hqk,khd->qhd', weights, value_rows, precision=HIGH_PRECISION)

def forward(source, w_qkv, w_out, w_fc, w_proj, attention_vectors, block_vectors, sizes):
    query_key_value_weight = w_qkv.reshape(D, 3 * D)
    output_weight = w_out.reshape(D, D)
    expand_full = w_fc.reshape(D + 1, FF)
    expand_weight = expand_full[:D]
    expand_bias = expand_full[D]
    contract_weight = w_proj.reshape(FF, D)
    token_rows = jnp.concatenate([attention_vectors, block_vectors]).reshape(8, D)
    first_normed = low(layer_norm(source, token_rows[0], token_rows[1]))
    mixed_heads = jnp.einsum('xbz,zn->xbn', first_normed, query_key_value_weight, precision=HIGH_PRECISION)
    query = low(low_back(mixed_heads[..., :D] + token_rows[2]))
    keys = low(low_back(mixed_heads[..., D:2 * D]))
    values = low(low_back(mixed_heads[..., 2 * D:] + token_rows[3]))
    shape = (source.shape[0], LENGTH, H, HD)

    def one_slot(item):
        return attend_slot(item[0], item[1], item[2], item[3])
    attention_output = lax.map(jax.checkpoint(one_slot), (query.reshape(shape), keys.reshape(shape), values.reshape(shape), sizes))
    attention_output = low(low_back(attention_output.reshape(source.shape)))
    residual_branch = low_back(jnp.einsum('xbz,zn->xbn', attention_output, output_weight, precision=HIGH_PRECISION) + token_rows[4])
    middle_state = source + residual_branch
    second_normed = low(layer_norm(middle_state, token_rows[5], token_rows[6]))
    inner_hidden = low_back(jnp.einsum('kgv,vy->kgy', second_normed, expand_weight, precision=HIGH_PRECISION) + expand_bias)
    active_tokens = low(tanh_gelu(inner_hidden))
    return middle_state + jnp.einsum('qan,nb->qab', active_tokens, contract_weight, precision=HIGH_PRECISION) + token_rows[7]

def reference(tokens, cotangent, lengths, w_qkv, w_out, w_fc, w_proj, attention_vectors, block_vectors):
    group = math.gcd(SLOTS, max(1, 4096 // LENGTH))
    blocks = SLOTS // group
    params = (w_qkv.astype(jnp.float32), w_out.astype(jnp.float32), w_fc.astype(jnp.float32), w_proj.astype(jnp.float32), attention_vectors.astype(jnp.float32), block_vectors.astype(jnp.float32))
    place = jnp.arange(LENGTH)

    def advance(totals, item):
        block, outer, sizes = item
        valid = (place[None, :] < sizes[:, None]).astype(jnp.float32)

        def runner(source, first, second, third, fourth, fifth, sixth):
            return forward(source, first, second, third, fourth, fifth, sixth, sizes)
        result, pullback = jax.vjp(runner, block.astype(jnp.float32), *params)
        grads = pullback(outer.astype(jnp.float32) * valid[..., None])
        sums = tuple((total + grad for total, grad in zip(totals, grads[1:])))
        return (sums, (result.astype(jnp.bfloat16), grads[0]))
    zeros_init = tuple((jnp.zeros_like(param) for param in params))
    totals, stacked = lax.scan(advance, zeros_init, (tokens.reshape(blocks, group, LENGTH, D), cotangent.reshape(blocks, group, LENGTH, D), lengths.reshape(blocks, group)))
    output = stacked[0].reshape(SLOTS, LENGTH, D)
    input_grad = stacked[1].reshape(SLOTS, LENGTH, D)
    return (output, input_grad, totals[0], totals[1], totals[2], totals[3], totals[4], totals[5])
```

```python
from functools import partial

import jax
import jax.numpy as jnp
from jax import lax
from jax.experimental import pallas as pl
from jax.experimental.pallas import tpu as pltpu
from jax.sharding import PartitionSpec as P

HD = 64
EPS = 1e-05
LANES = 128
BF = jnp.bfloat16
F32 = jnp.float32


def swap(value, axis, size, bit):
    return lax.ppermute(value, axis, [(i, i ^ bit) for i in range(size)])


def bits_of(size):
    return [1 << k for k in reversed(range(size.bit_length() - 1))]


def gather_relative(value, axis, size):
    pieces = {0: value}
    for bit in bits_of(size):
        for j in list(pieces):
            pieces[j ^ bit] = swap(pieces[j], axis, size, bit)
    return [pieces[j] for j in range(size)]


def gather_dp(value, size):
    if size > 8:
        return lax.all_gather(value, "dp", axis=0, tiled=False)
    mine = lax.axis_index("dp")
    out = jnp.zeros((size, *value.shape), value.dtype)
    for j, piece in enumerate(gather_relative(value, "dp", size)):
        out = lax.dynamic_update_index_in_dim(out, piece, mine ^ j, 0)
    return out


def scatter_dp(value, size):
    if size > 8:
        return lax.psum_scatter(value.astype(BF), "dp", scatter_dimension=0, tiled=False).astype(F32)
    mine = lax.axis_index("dp")
    bits = bits_of(size)
    value = value.reshape((2,) * len(bits) + value.shape[1:])
    for axis in reversed(range(len(bits))):
        bit = bits[axis]
        side = (mine // bit) % 2
        sent = lax.dynamic_index_in_dim(value, 1 - side, axis, keepdims=False).astype(BF)
        kept = lax.dynamic_index_in_dim(value, side, axis, keepdims=False)
        value = kept.astype(F32) + swap(sent, "dp", size, bit).astype(F32)
    return value


def scatter_seq(blocks, size):
    blocks = dict(enumerate(blocks))
    for bit in reversed(bits_of(size)):
        for j in sorted(blocks, reverse=True):
            if j & bit:
                got = swap(blocks.pop(j).astype(BF), "seq", size, bit)
                blocks[j ^ bit] = blocks[j ^ bit].astype(F32) + got.astype(F32)
    return blocks[0]


def pick(pieces, index):
    out = pieces[0]
    for k in range(1, len(pieces)):
        out = jnp.where(index == k, pieces[k], out)
    return out


def exchange_seq(pieces, size):
    mine = lax.axis_index("seq")
    got = []
    for j in range(size):
        sent = pick([pieces[b ^ j] for b in range(size)], mine)
        got.append(sent if j == 0 else swap(sent, "seq", size, j))
    return [pick([got[b ^ m] for m in range(size)], mine) for b in range(size)]


def pack_heads(value, size):
    rows, _, width = value.shape
    heads = width // HD
    own = -(-heads // size)
    value = jnp.pad(value.reshape(rows, 3, heads, HD), ((0, 0), (0, 0), (0, own * size - heads), (0, 0)))
    out = []
    for s in range(size):
        part = value[:, :, s * own : (s + 1) * own]
        even = own - own % 2
        cols = [part[:, :, :even].reshape(rows, -1)]
        if own % 2:
            cols += [part[:, :, even].reshape(rows, -1), jnp.zeros((rows, HD), value.dtype)]
        out.append(jnp.concatenate(cols, axis=1))
    return out


def unpack_heads(pieces, width):
    rows = pieces[0].shape[0]
    heads = width // HD
    own = -(-heads // len(pieces))
    even = own - own % 2
    out = []
    for piece in pieces:
        part = piece[:, : 3 * even * HD].reshape(rows, 3, even * HD)
        if own % 2:
            last = piece[:, 3 * even * HD : 3 * own * HD].reshape(rows, 3, HD)
            part = jnp.concatenate([part, last], axis=2)
        out.append(part)
    return jnp.concatenate(out, axis=2)[:, :, :width].reshape(rows, 3 * width)


def pack_hidden(value, size, dps):
    rows, hidden = value.shape
    value = value.reshape(rows, dps, size, hidden // (dps * size))
    return [value[:, :, s].reshape(rows, hidden // size) for s in range(size)]


def unpack_hidden(pieces, dps):
    rows, own = pieces[0].shape
    parts = [piece.reshape(rows, dps, 1, own // dps) for piece in pieces]
    return jnp.concatenate(parts, axis=2).reshape(rows, own * len(pieces))


def columns_from_rows(flat, rows, pack, size):
    cols = flat.shape[0] * size // rows
    if rows % size == 0:
        return jnp.concatenate(exchange_seq(pack(flat.reshape(rows // size, cols)), size), axis=0)
    full = lax.all_gather(flat, "seq", axis=0, tiled=True).reshape(rows, cols)
    return pick(pack(full), lax.axis_index("seq"))


def rows_from_columns(value, unpack, size):
    rows = value.shape[0]
    value = value.astype(BF)
    if rows % size == 0:
        part = rows // size
        return unpack(exchange_seq([value[b * part : (b + 1) * part] for b in range(size)], size)).reshape(-1)
    full = lax.all_gather(value, "seq", axis=0, tiled=False)
    full = unpack([full[b] for b in range(size)]).reshape(-1)
    count = full.shape[0] // size
    return lax.dynamic_slice_in_dim(full, lax.axis_index("seq") * count, count)


def half_masks():
    lane = lax.broadcasted_iota(jnp.int32, (1, LANES), 1)
    return [lane < HD, lane >= HD]


def row_block(ref, block, rows):
    return ref[pl.ds(pl.multiple_of(block * rows, rows), rows), :]


def attention_forward_kernel(size, pairs, odd, info, q_ref, k_ref, v_ref, o_ref, k_all, v_all):
    mine, length = info[0], info[1]
    count = q_ref.shape[0] // size
    pair = pl.program_id(0)
    last = pair == pairs - 1
    for a in range(size):
        rows = pl.ds(a * count, count)
        keys = row_block(k_ref, mine ^ a, count)
        if odd:
            keys = jnp.where(last, jnp.roll(keys, HD, axis=1), keys)
        k_all[rows, :] = keys
        v_all[rows, :] = row_block(v_ref, mine ^ a, count)
    halves = half_masks()
    zero = jnp.zeros((), BF)

    def one(a, half):
        span = (a + 1) * count
        q = jnp.where(half, row_block(q_ref, mine ^ a, count), zero)
        s = lax.dot_general(q, k_all[:span, :], (((1,), (1,)), ((), ())), preferred_element_type=F32) * 0.125
        limit = jnp.minimum(a * count + lax.broadcasted_iota(jnp.int32, (count, 1), 0), length - 1)
        allowed = lax.broadcasted_iota(jnp.int32, (count, span), 1) <= limit
        s = jnp.where(allowed, s, -1e30)
        e = jnp.exp(s - jnp.max(s, axis=1, keepdims=True))
        p = (e * (1.0 / jnp.sum(e, axis=1, keepdims=True))).astype(BF)
        return jnp.dot(p, v_all[:span, :], preferred_element_type=F32)

    for a in range(size):
        rows = pl.ds(pl.multiple_of((mine ^ a) * count, count), count)
        first = one(a, halves[0])
        if not odd:
            o_ref[rows, :] = jnp.where(halves[0], first, one(a, halves[1])).astype(BF)
            continue
        o_ref[rows, :] = jnp.where(halves[0], first, 0.0).astype(BF)

        @pl.when(jnp.logical_not(last))
        def _():
            o_ref[rows, :] = jnp.where(halves[0], o_ref[rows, :], one(a, halves[1]).astype(BF))


def attention_backward_kernel(size, pairs, odd, info, q_ref, k_ref, v_ref, g_ref, d_ref, k_all, v_all, dq, dk, dv):
    mine, length = info[0], info[1]
    count = q_ref.shape[0] // size
    pair = pl.program_id(0)
    last = pair == pairs - 1
    for a in range(size):
        rows = pl.ds(a * count, count)
        keys = row_block(k_ref, mine ^ a, count)
        if odd:
            keys = jnp.where(last, jnp.roll(keys, HD, axis=1), keys)
        k_all[rows, :] = keys
        v_all[rows, :] = row_block(v_ref, mine ^ a, count)
    dk[...] = jnp.zeros_like(dk)
    dv[...] = jnp.zeros_like(dv)
    halves = half_masks()
    zero = jnp.zeros((), BF)

    def one(a, which):
        half = halves[which]
        span = (a + 1) * count
        rows = pl.ds(a * count, count)
        q = jnp.where(half, row_block(q_ref, mine ^ a, count), zero)
        g = jnp.where(half, row_block(g_ref, mine ^ a, count), zero)
        keys, values = k_all[:span, :], v_all[:span, :]
        contract = (((1,), (1,)), ((), ()))
        s = lax.dot_general(keys, q, contract, preferred_element_type=F32) * 0.125
        limit = jnp.minimum(a * count + lax.broadcasted_iota(jnp.int32, (1, count), 1), length - 1)
        allowed = lax.broadcasted_iota(jnp.int32, (span, count), 0) <= limit
        s = jnp.where(allowed, s, -1e30)
        e = jnp.exp(s - jnp.max(s, axis=0, keepdims=True))
        p = e * (1.0 / jnp.sum(e, axis=0, keepdims=True))
        dp = lax.dot_general(values, g, contract, preferred_element_type=F32)
        inner = jnp.sum(p * dp, axis=0, keepdims=True)
        ds = (p * (dp - inner) * 0.125).astype(BF)
        dv[:span, :] += jnp.dot(p.astype(BF), g, preferred_element_type=F32)
        dk[:span, :] += jnp.dot(ds, q, preferred_element_type=F32)
        part = lax.dot_general(ds, keys, (((0,), (0,)), ((), ())), preferred_element_type=F32)
        if which == 0:
            dq[rows, :] = jnp.where(half, part, 0.0)
        else:
            dq[rows, :] = jnp.where(half, part, dq[rows, :])

    for a in range(size):
        one(a, 0)
    if odd:

        @pl.when(jnp.logical_not(last))
        def _():
            for a in range(size):
                one(a, 1)
    else:
        for a in range(size):
            one(a, 1)

    def store(block, value_of):
        cols = pl.ds(pl.multiple_of(block * LANES, LANES), LANES)
        for a in range(size):
            rows = pl.ds(pl.multiple_of((mine ^ a) * count, count), count)
            d_ref[rows, cols] = value_of(pl.ds(a * count, count)).astype(BF)

    full = pairs - 1 if odd else pairs

    def plain():
        store(pair, lambda r: dq[r, :])
        store(full + pair, lambda r: dk[r, :])
        store(2 * full + pair, lambda r: dv[r, :])

    if not odd:
        plain()
        return
    pl.when(jnp.logical_not(last))(plain)

    @pl.when(last)
    def _():
        store(3 * full, lambda r: jnp.where(halves[0], dq[r, :], jnp.roll(dk[r, :], HD, axis=1)))
        store(3 * full + 1, lambda r: jnp.where(halves[0], dv[r, :], 0.0))


def head_specs(span, pairs, odd):
    full = pairs - 1 if odd else pairs

    def spec(part):
        def index(j, info):
            if not odd:
                return (0, part * full + j)
            return (0, jnp.where(j < full, part * full + j, 3 * full + (part == 2)))

        return pl.BlockSpec((span, LANES), index)

    return [spec(0), spec(1), spec(2)]


def attention_forward(info, mixed, own, size):
    span = mixed.shape[0]
    pairs, odd = -(-own // 2), own % 2
    return pl.pallas_call(
        partial(attention_forward_kernel, size, pairs, odd),
        out_shape=jax.ShapeDtypeStruct((span, pairs * LANES), BF),
        grid_spec=pltpu.PrefetchScalarGridSpec(
            num_scalar_prefetch=1,
            grid=(pairs,),
            in_specs=head_specs(span, pairs, odd),
            out_specs=pl.BlockSpec((span, LANES), lambda j, info: (0, j)),
            scratch_shapes=[pltpu.VMEM((span, LANES), BF)] * 2,
        ),
        compiler_params=pltpu.CompilerParams(vmem_limit_bytes=40 << 20),
        cost_estimate=pl.CostEstimate(
            flops=own * span * span * 256, transcendentals=own * span * span // 2, bytes_accessed=mixed.size * 4
        ),
        name="attention_forward",
    )(info, mixed, mixed, mixed)


def attention_backward(info, mixed, grad, own, size):
    span = mixed.shape[0]
    pairs, odd = -(-own // 2), own % 2
    return pl.pallas_call(
        partial(attention_backward_kernel, size, pairs, odd),
        out_shape=jax.ShapeDtypeStruct(mixed.shape, BF),
        grid_spec=pltpu.PrefetchScalarGridSpec(
            num_scalar_prefetch=1,
            grid=(pairs,),
            in_specs=[*head_specs(span, pairs, odd), pl.BlockSpec((span, LANES), lambda j, info: (0, j))],
            out_specs=pl.BlockSpec(mixed.shape, lambda j, info: (0, 0)),
            scratch_shapes=[pltpu.VMEM((span, LANES), BF)] * 2 + [pltpu.VMEM((span, LANES), F32)] * 3,
        ),
        compiler_params=pltpu.CompilerParams(vmem_limit_bytes=48 << 20),
        cost_estimate=pl.CostEstimate(
            flops=own * span * span * 768, transcendentals=own * span * span // 2, bytes_accessed=mixed.size * 6
        ),
        name="attention_backward",
    )(info, mixed, mixed, mixed, grad)


def normal(value):
    centre = value - jnp.mean(value, axis=-1, keepdims=True)
    scale = lax.rsqrt(jnp.mean(centre * centre, axis=-1, keepdims=True) + EPS)
    return centre * scale, scale


def norm_input_grad(unit, scale, gain, grad):
    scaled = grad * gain
    return scale * (
        scaled
        - jnp.mean(scaled, axis=-1, keepdims=True)
        - unit * jnp.mean(scaled * unit, axis=-1, keepdims=True)
    )


ROOT = 0.7978845608028654
CUBIC = 0.044715


def gelu(u):
    return 0.5 * u * (1.0 + jnp.tanh(ROOT * (u + CUBIC * u * u * u)))


def gelu_slope(u):
    t = jnp.tanh(ROOT * (u + CUBIC * u * u * u))
    return 0.5 * (1.0 + t) + 0.5 * u * (1.0 - t * t) * ROOT * (1.0 + 3.0 * CUBIC * u * u)


def dot(a, b, dims=((1,), (0,))):
    return lax.dot_general(a, b, (dims, ((), ())), preferred_element_type=F32)


def local(size, dps, tokens, cotangent, lengths, w_qkv, w_out, w_fc, w_proj, attention_vectors, block_vectors):
    _, count, width = tokens.shape
    heads = width // HD
    own = -(-heads // size)
    hidden = w_proj.shape[0] * dps * size // width
    rank = lax.axis_index("seq")
    row = lax.axis_index("dp")
    device = row * size + rank
    devices = dps * size
    length = lengths[0]
    info = jnp.stack([rank.astype(jnp.int32), length])
    unit_rows = width // dps

    vectors = lax.all_gather(jnp.stack([attention_vectors, block_vectors]), ("dp", "seq"), axis=1, tiled=True)
    vectors = vectors.astype(F32).reshape(8, width)
    gain1, shift1, bias_q, bias_v, bias_o, gain2, shift2, bias_p = (vectors[k] for k in range(8))

    x_own = tokens[0]
    x_all = jnp.concatenate(gather_relative(x_own, "seq", size), axis=0)
    place = rank * count + jnp.arange(count)
    dy_own = cotangent[0] * (place < length).astype(BF)[:, None]

    pack3 = lambda m: pack_heads(m.reshape(m.shape[0], 3, width), size)
    qkv_part = columns_from_rows(w_qkv, unit_rows, pack3, size)
    qkv_full = gather_dp(qkv_part, dps).reshape(width, -1)

    out_parts = gather_dp(w_out, dps)
    out_parts = gather_relative(out_parts, "seq", size)
    out_full = jnp.stack([pick([out_parts[b ^ m] for m in range(size)], rank) for b in range(size)], axis=1)
    out_full = out_full.reshape(width, width)

    shift = hidden // devices
    tail = -(-shift * devices // LANES) * LANES
    plain = w_fc.shape[0] - shift
    before = lax.ppermute(w_fc[-tail:], ("dp", "seq"), [(i, i + 1) for i in range(devices - 1)])
    fc_flat = lax.dynamic_slice_in_dim(jnp.concatenate([before, w_fc]), tail - shift * device, plain)
    bias_rows = lax.psum(jnp.where(device == devices - 1, w_fc[-hidden:], jnp.zeros((), BF)).astype(F32), ("dp", "seq"))
    pack_fc = lambda m: pack_hidden(m, size, dps)
    fc_part = columns_from_rows(fc_flat, unit_rows, pack_fc, size)
    fc_full = gather_dp(fc_part, dps).reshape(width, -1)
    bias_fc = pick(pack_fc(bias_rows[None]), rank)

    proj_full = gather_dp(w_proj.reshape(-1, width), dps).reshape(-1, width)

    unit1_all, _ = normal(x_all.astype(F32))
    h1 = (unit1_all * gain1 + shift1).astype(BF)
    bias_qkv = pick(pack3(jnp.stack([bias_q, jnp.zeros_like(bias_q), bias_v])[None]), rank)
    mixed = (dot(h1, qkv_full) + bias_qkv).astype(BF)
    o_heads = attention_forward(info, mixed, own, size)
    o_got = [o_heads[:count]] + [
        swap(o_heads[j * count : (j + 1) * count], "seq", size, j) for j in range(1, size)
    ]
    o_own = jnp.concatenate([pick([o_got[b ^ m] for m in range(size)], rank)[:, : own * HD] for b in range(size)], axis=1)
    o_own = o_own[:, :width]
    x2 = x_own.astype(F32) + dot(o_own, out_full) + bias_o
    unit2, scale2 = normal(x2)
    h2_own = (unit2 * gain2 + shift2).astype(BF)
    h2 = jnp.concatenate(gather_relative(h2_own, "seq", size), axis=0)
    dy = jnp.concatenate(gather_relative(dy_own, "seq", size), axis=0)
    u = dot(h2, fc_full) + bias_fc
    a = gelu(u).astype(BF)
    split = lambda m: [m[j * count : (j + 1) * count] for j in range(size)]
    output = (x2 + scatter_seq(split(dot(a, proj_full)), size) + bias_p).astype(BF)

    dy_wide = dy_own.astype(F32)
    grad_proj = scatter_dp(dot(a, dy, ((0,), (0,))).reshape(dps, -1, width), dps).reshape(-1)
    grad_bp = jnp.sum(dy_wide, axis=0)
    du = (dot(dy, proj_full, ((1,), (1,))) * gelu_slope(u)).astype(BF)
    grad_bf = jnp.sum(du.astype(F32), axis=0)
    dh2 = scatter_seq(split(dot(du, fc_full, ((1,), (1,)))), size)
    grad_fc = scatter_dp(dot(h2, du, ((0,), (0,))).reshape(dps, unit_rows, -1), dps)
    grad_g2 = jnp.sum(dh2 * unit2, axis=0)
    grad_c2 = jnp.sum(dh2, axis=0)
    dx2 = dy_wide + norm_input_grad(unit2, scale2, gain2, dh2)
    dz = dx2.astype(BF)
    grad_bo = jnp.sum(dz.astype(F32), axis=0)

    do_own = jnp.pad(dot(dz, out_full, ((1,), (1,))).astype(BF), ((0, 0), (0, own * size * HD - width)))
    do_blocks = [jnp.pad(do_own[:, b * own * HD : (b + 1) * own * HD], ((0, 0), (0, own % 2 * HD))) for b in range(size)]
    do_got = []
    for j in range(size):
        sent = pick([do_blocks[b ^ j] for b in range(size)], rank)
        do_got.append(sent if j == 0 else swap(sent, "seq", size, j))
    do_heads = jnp.concatenate(do_got, axis=0)
    grad_out = dot(o_own, dz, ((0,), (0,)))
    grad_out = grad_out.reshape((dps, size, -1, width) if width % devices == 0 else (dps, size, -1))
    grad_out = scatter_seq([lax.dynamic_index_in_dim(grad_out, rank ^ j, 1, keepdims=False) for j in range(size)], size)
    grad_out = scatter_dp(grad_out, dps).reshape(-1)
    dmixed = attention_backward(info, mixed, do_heads, own, size)
    grad_mixed = jnp.sum(dmixed.astype(F32), axis=0)
    dh1_part = dot(dmixed, qkv_full, ((1,), (1,)))
    grad_c1 = jnp.sum(dh1_part, axis=0)
    grad_g1 = jnp.sum(dh1_part * unit1_all, axis=0)
    dh1 = scatter_seq(split(dh1_part), size)
    grad_qkv = scatter_dp(dot(h1, dmixed, ((0,), (0,))).reshape(dps, unit_rows, -1), dps)
    unit1, scale1 = normal(x_own.astype(F32))
    input_grad = dx2 + norm_input_grad(unit1, scale1, gain1, dh1)

    place_cols = lambda v, pack_size, unpack: unpack([jnp.where(rank == b, v, 0.0)[None] for b in range(pack_size)])[0]
    wide = place_cols(grad_mixed, size, lambda p: unpack_heads(p, width)).reshape(3, width)
    wide_bf = place_cols(grad_bf, size, lambda p: unpack_hidden(p, dps))
    sums = jnp.concatenate(
        [grad_g1, grad_c1, wide[0], wide[2], grad_bo, grad_g2, grad_c2, grad_bp, wide_bf]
    )
    sums = lax.psum(sums, ("dp", "seq"))
    part = attention_vectors.shape[0]
    vec1 = lax.dynamic_slice_in_dim(sums[: 4 * width], device * part, part)
    vec2 = lax.dynamic_slice_in_dim(sums[4 * width : 8 * width], device * part, part)
    sum_bf = sums[8 * width :]

    qkv_flat = rows_from_columns(grad_qkv, lambda p: unpack_heads(p, width), size).astype(F32)
    fc_rows = rows_from_columns(grad_fc, lambda p: unpack_hidden(p, dps), size)
    after = lax.ppermute(fc_rows[:tail], ("dp", "seq"), [(i + 1, i) for i in range(devices - 1)])
    fill = jnp.pad(sum_bf, (0, tail - hidden))
    after = jnp.where(device == devices - 1, fill, after.astype(F32))
    fc_flat_grad = lax.dynamic_slice_in_dim(
        jnp.concatenate([fc_rows.astype(F32), after]), shift * device, w_fc.shape[0]
    )
    return (output[None], input_grad[None], qkv_flat, grad_out, fc_flat_grad, grad_proj, vec1, vec2)


def solution(mesh):
    tokens = P("dp", "seq", None)
    flat = P(("dp", "seq"))
    return jax.shard_map(
        partial(local, mesh.shape["seq"], mesh.shape["dp"]),
        mesh=mesh,
        in_specs=(tokens, tokens, P("dp"), *[flat] * 6),
        out_specs=(tokens, tokens, *[flat] * 6),
        check_vma=False,
    )
```

```python
from functools import partial

import jax
import jax.numpy as jnp
from jax import lax
from jax.experimental import pallas as pl
from jax.experimental.pallas import tpu as pltpu
from jax.sharding import PartitionSpec as P

HD = 64
EPS = 1e-05
LANES = 128
BF = jnp.bfloat16
F32 = jnp.float32


def bits_of(size):
    return [1 << k for k in reversed(range(size.bit_length() - 1))]


def after(value, *others):
    others = [o for o in others if o is not None]
    return lax.optimization_barrier((value, *others))[0] if others else value


def pick(pieces, index):
    out = pieces[0]
    for k in range(1, len(pieces)):
        out = jnp.where(index == k, pieces[k], out)
    return out


class Links:
    def __init__(self, dps, seqs):
        self.sizes = {"dp": dps, "seq": seqs}
        self.last = {}

    def ordered(self, value, link, permute):
        self.last[link] = permute(after(value, self.last.get(link)))
        return self.last[link]

    def swap(self, value, axis, bits):
        pairs = [(i, i ^ bits) for i in range(self.sizes[axis])]
        top = 1 << (bits.bit_length() - 1)
        return self.ordered(value, (axis, top), lambda v: lax.ppermute(v, axis, pairs))

    def shift(self, value, step):
        count = self.sizes["dp"] * self.sizes["seq"]
        pairs = [(i, i + step) for i in range(count) if 0 <= i + step < count]
        return self.ordered(value, ("seq", 1), lambda v: lax.ppermute(v, ("dp", "seq"), pairs))

    def all_sum(self, value, axes):
        for axis in axes:
            for bit in bits_of(self.sizes[axis]):
                value = value + self.swap(value, axis, bit)
        return value

    def gather_seq(self, value):
        pieces = {0: value}
        for bit in bits_of(self.sizes["seq"]):
            for j in list(pieces):
                pieces[j ^ bit] = self.swap(pieces[j], "seq", bit)
        return [pieces[j] for j in range(len(pieces))]

    def scatter_seq(self, blocks):
        blocks = dict(enumerate(blocks))
        for bit in reversed(bits_of(self.sizes["seq"])):
            for j in sorted(blocks, reverse=True):
                if j & bit:
                    got = self.swap(blocks.pop(j).astype(BF), "seq", bit)
                    blocks[j ^ bit] = blocks[j ^ bit].astype(F32) + got.astype(F32)
        return blocks[0]

    def exchange_seq(self, pieces):
        return [pieces[0]] + [self.swap(pieces[j], "seq", j) for j in range(1, len(pieces))]

    def relative(self, pieces, axis="seq"):
        mine, size = lax.axis_index(axis), len(pieces)
        return [pick([pieces[j ^ m] for m in range(size)], mine) for j in range(size)]

    def columns_from_rows(self, flat, rows, pack):
        size = self.sizes["seq"]
        cols = flat.shape[0] * size // rows
        if rows % size == 0:
            pieces = self.relative(pack(flat.reshape(rows // size, cols)))
            return jnp.concatenate(self.relative(self.exchange_seq(pieces)), axis=0)
        full = lax.all_gather(flat, "seq", axis=0, tiled=True).reshape(rows, cols)
        return pick(pack(full), lax.axis_index("seq"))

    def rows_from_columns(self, value, unpack):
        size = self.sizes["seq"]
        rows = value.shape[0]
        value = value.astype(BF)
        if rows % size == 0:
            part = rows // size
            pieces = self.relative([value[b * part : (b + 1) * part] for b in range(size)])
            return unpack(self.relative(self.exchange_seq(pieces))).reshape(-1)
        full = lax.all_gather(value, "seq", axis=0, tiled=False)
        full = unpack([full[b] for b in range(size)]).reshape(-1)
        count = full.shape[0] // size
        return lax.dynamic_slice_in_dim(full, lax.axis_index("seq") * count, count)


def block(value, j):
    return lax.dynamic_index_in_dim(value, lax.axis_index("dp") ^ j, 0, keepdims=False)


class Ring:
    def __init__(self, size):
        self.size = size
        self.order = [*range(0, size, 2), *range(size - 1, 0, -2)] if size == 8 else list(range(size))
        self.groups = [self.order] if size == 8 else None

    def gather(self, value):
        return lax.all_gather(value, "dp", axis=0, tiled=True, axis_index_groups=self.groups)

    def scatter(self, value):
        total = lax.psum_scatter(value, "dp", scatter_dimension=0, tiled=True, axis_index_groups=self.groups)
        return lax.optimization_barrier(total).astype(F32)

    def inward(self, value):
        return self.blocks(value, self.order)

    def outward(self, value):
        return self.blocks(value, [self.order.index(d) for d in range(self.size)])

    def blocks(self, value, order):
        if self.groups is None:
            return value
        part = value.shape[-1] // self.size
        return jnp.concatenate([value[..., d * part : (d + 1) * part] for d in order], axis=-1)


def pack_heads(value, size):
    rows, _, width = value.shape
    heads = width // HD
    own = -(-heads // size)
    value = jnp.pad(value.reshape(rows, 3, heads, HD), ((0, 0), (0, 0), (0, own * size - heads), (0, 0)))
    out = []
    for s in range(size):
        part = value[:, :, s * own : (s + 1) * own]
        even = own - own % 2
        cols = [part[:, :, :even].reshape(rows, -1)]
        if own % 2:
            cols += [part[:, :, even].reshape(rows, -1), jnp.zeros((rows, HD), value.dtype)]
        out.append(jnp.concatenate(cols, axis=1))
    return out


def unpack_heads(pieces, width):
    rows = pieces[0].shape[0]
    heads = width // HD
    own = -(-heads // len(pieces))
    even = own - own % 2
    out = []
    for piece in pieces:
        part = piece[:, : 3 * even * HD].reshape(rows, 3, even * HD)
        if own % 2:
            last = piece[:, 3 * even * HD : 3 * own * HD].reshape(rows, 3, HD)
            part = jnp.concatenate([part, last], axis=2)
        out.append(part)
    return jnp.concatenate(out, axis=2)[:, :, :width].reshape(rows, 3 * width)


def pack_hidden(value, size, order):
    rows, hidden = value.shape
    value = value.reshape(rows, len(order), size, hidden // (len(order) * size))
    return [jnp.concatenate([value[:, d, s] for d in order], axis=1) for s in range(size)]


def unpack_hidden(pieces, order):
    rows, own = pieces[0].shape
    part = own // len(order)
    cut = lambda piece, k: piece[:, k * part : (k + 1) * part]
    return jnp.concatenate([cut(piece, order.index(d)) for d in range(len(order)) for piece in pieces], axis=1)


def half_masks():
    lane = lax.broadcasted_iota(jnp.int32, (1, LANES), 1)
    return [lane < HD, lane >= HD]


def row_block(ref, block, rows):
    return ref[pl.ds(pl.multiple_of(block * rows, rows), rows), :]


def attention_forward_kernel(size, pairs, odd, info, q_ref, k_ref, v_ref, o_ref, k_all, v_all):
    mine, length = info[0], info[1]
    count = q_ref.shape[0] // size
    pair = pl.program_id(0)
    last = pair == pairs - 1
    for a in range(size):
        rows = pl.ds(a * count, count)
        keys = row_block(k_ref, mine ^ a, count)
        if odd:
            keys = jnp.where(last, jnp.roll(keys, HD, axis=1), keys)
        k_all[rows, :] = keys
        v_all[rows, :] = row_block(v_ref, mine ^ a, count)
    halves = half_masks()
    zero = jnp.zeros((), BF)

    def one(a, half):
        span = (a + 1) * count
        q = jnp.where(half, row_block(q_ref, mine ^ a, count), zero)
        s = lax.dot_general(q, k_all[:span, :], (((1,), (1,)), ((), ())), preferred_element_type=F32) * 0.125
        limit = jnp.minimum(a * count + lax.broadcasted_iota(jnp.int32, (count, 1), 0), length - 1)
        allowed = lax.broadcasted_iota(jnp.int32, (count, span), 1) <= limit
        s = jnp.where(allowed, s, -1e30)
        e = jnp.exp(s - jnp.max(s, axis=1, keepdims=True))
        p = (e * (1.0 / jnp.sum(e, axis=1, keepdims=True))).astype(BF)
        return jnp.dot(p, v_all[:span, :], preferred_element_type=F32)

    for a in range(size):
        rows = pl.ds(pl.multiple_of((mine ^ a) * count, count), count)
        first = one(a, halves[0])
        if not odd:
            o_ref[rows, :] = jnp.where(halves[0], first, one(a, halves[1])).astype(BF)
            continue
        o_ref[rows, :] = jnp.where(halves[0], first, 0.0).astype(BF)

        @pl.when(jnp.logical_not(last))
        def _():
            o_ref[rows, :] = jnp.where(halves[0], o_ref[rows, :], one(a, halves[1]).astype(BF))


def attention_backward_kernel(size, pairs, odd, info, q_ref, k_ref, v_ref, g_ref, d_ref, k_all, v_all, dq, dk, dv):
    mine, length = info[0], info[1]
    count = q_ref.shape[0] // size
    pair = pl.program_id(0)
    last = pair == pairs - 1
    for a in range(size):
        rows = pl.ds(a * count, count)
        keys = row_block(k_ref, mine ^ a, count)
        if odd:
            keys = jnp.where(last, jnp.roll(keys, HD, axis=1), keys)
        k_all[rows, :] = keys
        v_all[rows, :] = row_block(v_ref, mine ^ a, count)
    dk[...] = jnp.zeros_like(dk)
    dv[...] = jnp.zeros_like(dv)
    halves = half_masks()
    zero = jnp.zeros((), BF)

    def one(a, which):
        half = halves[which]
        span = (a + 1) * count
        rows = pl.ds(a * count, count)
        q = jnp.where(half, row_block(q_ref, mine ^ a, count), zero)
        g = jnp.where(half, row_block(g_ref, mine ^ a, count), zero)
        keys, values = k_all[:span, :], v_all[:span, :]
        contract = (((1,), (1,)), ((), ()))
        s = lax.dot_general(keys, q, contract, preferred_element_type=F32) * 0.125
        limit = jnp.minimum(a * count + lax.broadcasted_iota(jnp.int32, (1, count), 1), length - 1)
        allowed = lax.broadcasted_iota(jnp.int32, (span, count), 0) <= limit
        s = jnp.where(allowed, s, -1e30)
        e = jnp.exp(s - jnp.max(s, axis=0, keepdims=True))
        p = e * (1.0 / jnp.sum(e, axis=0, keepdims=True))
        dp = lax.dot_general(values, g, contract, preferred_element_type=F32)
        inner = jnp.sum(p * dp, axis=0, keepdims=True)
        ds = (p * (dp - inner) * 0.125).astype(BF)
        dv[:span, :] += jnp.dot(p.astype(BF), g, preferred_element_type=F32)
        dk[:span, :] += jnp.dot(ds, q, preferred_element_type=F32)
        part = lax.dot_general(ds, keys, (((0,), (0,)), ((), ())), preferred_element_type=F32)
        if which == 0:
            dq[rows, :] = jnp.where(half, part, 0.0)
        else:
            dq[rows, :] = jnp.where(half, part, dq[rows, :])

    for a in range(size):
        one(a, 0)
    if odd:

        @pl.when(jnp.logical_not(last))
        def _():
            for a in range(size):
                one(a, 1)
    else:
        for a in range(size):
            one(a, 1)

    def store(block, value_of):
        cols = pl.ds(pl.multiple_of(block * LANES, LANES), LANES)
        for a in range(size):
            rows = pl.ds(pl.multiple_of((mine ^ a) * count, count), count)
            d_ref[rows, cols] = value_of(pl.ds(a * count, count)).astype(BF)

    full = pairs - 1 if odd else pairs

    def plain():
        store(pair, lambda r: dq[r, :])
        store(full + pair, lambda r: dk[r, :])
        store(2 * full + pair, lambda r: dv[r, :])

    if not odd:
        plain()
        return
    pl.when(jnp.logical_not(last))(plain)

    @pl.when(last)
    def _():
        store(3 * full, lambda r: jnp.where(halves[0], dq[r, :], jnp.roll(dk[r, :], HD, axis=1)))
        store(3 * full + 1, lambda r: jnp.where(halves[0], dv[r, :], 0.0))


def head_specs(span, pairs, odd):
    full = pairs - 1 if odd else pairs

    def spec(part):
        def index(j, info):
            if not odd:
                return (0, part * full + j)
            return (0, jnp.where(j < full, part * full + j, 3 * full + (part == 2)))

        return pl.BlockSpec((span, LANES), index)

    return [spec(0), spec(1), spec(2)]


def attention_forward(info, mixed, own, size):
    span = mixed.shape[0]
    pairs, odd = -(-own // 2), own % 2
    return pl.pallas_call(
        partial(attention_forward_kernel, size, pairs, odd),
        out_shape=jax.ShapeDtypeStruct((span, pairs * LANES), BF),
        grid_spec=pltpu.PrefetchScalarGridSpec(
            num_scalar_prefetch=1,
            grid=(pairs,),
            in_specs=head_specs(span, pairs, odd),
            out_specs=pl.BlockSpec((span, LANES), lambda j, info: (0, j)),
            scratch_shapes=[pltpu.VMEM((span, LANES), BF)] * 2,
        ),
        compiler_params=pltpu.CompilerParams(vmem_limit_bytes=40 << 20),
        cost_estimate=pl.CostEstimate(
            flops=own * span * span * 256, transcendentals=own * span * span // 2, bytes_accessed=mixed.size * 4
        ),
        name="attention_forward",
    )(info, mixed, mixed, mixed)


def attention_backward(info, mixed, grad, own, size):
    span = mixed.shape[0]
    pairs, odd = -(-own // 2), own % 2
    return pl.pallas_call(
        partial(attention_backward_kernel, size, pairs, odd),
        out_shape=jax.ShapeDtypeStruct(mixed.shape, BF),
        grid_spec=pltpu.PrefetchScalarGridSpec(
            num_scalar_prefetch=1,
            grid=(pairs,),
            in_specs=[*head_specs(span, pairs, odd), pl.BlockSpec((span, LANES), lambda j, info: (0, j))],
            out_specs=pl.BlockSpec(mixed.shape, lambda j, info: (0, 0)),
            scratch_shapes=[pltpu.VMEM((span, LANES), BF)] * 2 + [pltpu.VMEM((span, LANES), F32)] * 3,
        ),
        compiler_params=pltpu.CompilerParams(vmem_limit_bytes=48 << 20),
        cost_estimate=pl.CostEstimate(
            flops=own * span * span * 768, transcendentals=own * span * span // 2, bytes_accessed=mixed.size * 6
        ),
        name="attention_backward",
    )(info, mixed, mixed, mixed, grad)


def normal(value):
    centre = value - jnp.mean(value, axis=-1, keepdims=True)
    scale = lax.rsqrt(jnp.mean(centre * centre, axis=-1, keepdims=True) + EPS)
    return centre * scale, scale


def norm_input_grad(unit, scale, gain, grad):
    scaled = grad * gain
    return scale * (
        scaled
        - jnp.mean(scaled, axis=-1, keepdims=True)
        - unit * jnp.mean(scaled * unit, axis=-1, keepdims=True)
    )


ROOT = 0.7978845608028654
CUBIC = 0.044715


def gelu(u):
    return 0.5 * u * (1.0 + jnp.tanh(ROOT * (u + CUBIC * u * u * u)))


def gelu_slope(u):
    t = jnp.tanh(ROOT * (u + CUBIC * u * u * u))
    return 0.5 * (1.0 + t) + 0.5 * u * (1.0 - t * t) * ROOT * (1.0 + 3.0 * CUBIC * u * u)


def dot(a, b, dims=((1,), (0,))):
    return lax.dot_general(a, b, (dims, ((), ())), preferred_element_type=F32)


def local(size, dps, tokens, cotangent, lengths, w_qkv, w_out, w_fc, w_proj, attention_vectors, block_vectors):
    _, count, width = tokens.shape
    heads = width // HD
    own = -(-heads // size)
    hidden = w_proj.shape[0] * dps * size // width
    rank = lax.axis_index("seq")
    row = lax.axis_index("dp")
    device = row * size + rank
    devices = dps * size
    length = lengths[0]
    info = jnp.stack([rank.astype(jnp.int32), length])
    unit_rows = width // dps

    links = Links(dps, size)

    pack3 = lambda m: pack_heads(m.reshape(m.shape[0], 3, width), size)
    ring = Ring(dps)
    pack_fc = lambda m: pack_hidden(m, size, ring.order)
    unpack_fc = lambda p: unpack_hidden(p, ring.order)

    split = lambda m: [m[j * count : (j + 1) * count] for j in range(size)]

    aligned = unit_rows % 8 == 0 and unit_rows % size == 0
    rows = unit_rows // size
    if aligned:
        starts = [rows * b // 8 * 8 for b in range(size)]
        window = max(-(-(rows * (b + 1) - starts[b]) // 8) * 8 for b in range(size))
        starts = [min(start, unit_rows - window) for start in starts]
        starts = [pl.multiple_of(v, 8) for v in links.relative([jnp.int32(v) for v in starts])]
        pieces = jnp.concatenate(links.relative(links.gather_seq(ring.inward(w_out.reshape(rows, width)))), axis=0)
        out_part = ring.gather(lax.dynamic_slice_in_dim(pieces, starts[0], window, 0)).reshape(dps, window, width)
    else:
        out_part = lax.all_gather(w_out, "dp", axis=0, tiled=False)
    qkv_part = links.columns_from_rows(w_qkv, unit_rows, pack3)
    qkv_full = ring.gather(qkv_part)

    shift = hidden // devices
    tail = -(-shift * devices // LANES) * LANES
    before = links.shift(w_fc[-tail:], 1)
    part = attention_vectors.shape[0]
    last = device == devices - 1
    small = jnp.zeros((8 * width,), BF)
    small = lax.dynamic_update_slice_in_dim(small, attention_vectors, device * part, 0)
    small = lax.dynamic_update_slice_in_dim(small, block_vectors, 4 * width + device * part, 0)
    small = jnp.concatenate([small, jnp.where(last, w_fc[-hidden:], jnp.zeros((), BF))])
    small = links.all_sum(small, ("seq", "dp")).astype(F32)
    gain1, shift1, bias_q, bias_v, bias_o, gain2, shift2, bias_p = (small[k * width : (k + 1) * width] for k in range(8))
    gain1, shift1, bias_o, gain2, shift2, bias_p = (ring.inward(v) for v in (gain1, shift1, bias_o, gain2, shift2, bias_p))
    bias_fc = pick(pack_fc(small[None, 8 * width :]), rank)
    bias_qkv = pick(pack3(jnp.stack([bias_q, jnp.zeros_like(bias_q), bias_v])[None]), rank)

    x_own = ring.inward(tokens[0])
    x_all = jnp.concatenate(links.gather_seq(x_own), axis=0)
    plain = w_fc.shape[0] - shift
    fc_flat = lax.dynamic_slice_in_dim(jnp.concatenate([before, after(w_fc, small)]), tail - shift * device, plain)
    fc_part = links.columns_from_rows(fc_flat, unit_rows, pack_fc)
    fc_full = ring.gather(fc_part)

    out_parts = links.gather_seq(out_part)

    unit1_all, _ = normal(x_all.astype(F32))
    h1 = (unit1_all * gain1 + shift1).astype(BF)
    mixed = (dot(h1, qkv_full) + bias_qkv).astype(BF)
    proj_full = ring.gather(after(ring.inward(w_proj.reshape(-1, width)), fc_part, mixed))
    place = rank * count + jnp.arange(count)
    dy_own = ring.inward(cotangent[0]) * (place < length).astype(BF)[:, None]
    dy_wide = dy_own.astype(F32)
    dy = jnp.concatenate(links.gather_seq(after(dy_own, mixed)), axis=0)
    o_heads = attention_forward(info, mixed, own, size)
    out_parts = [after(piece, mixed) for piece in out_parts]
    if aligned:
        out_full = jnp.zeros((dps, unit_rows, width), BF)
        for j in range(size):
            out_full = lax.dynamic_update_slice_in_dim(out_full, out_parts[j], starts[j], 1)
    else:
        out_full = jnp.stack(links.relative(out_parts), axis=1)
    out_full = out_full.reshape(width, width)

    o_got = links.relative(links.exchange_seq(split(o_heads)))
    o_own = jnp.concatenate([piece[:, : own * HD] for piece in o_got], axis=1)
    o_own = ring.inward(o_own[:, :width])
    x2 = x_own.astype(F32) + dot(o_own, out_full) + bias_o
    unit2, scale2 = normal(x2)
    h2 = jnp.concatenate(links.gather_seq((unit2 * gain2 + shift2).astype(BF)), axis=0)

    u = dot(h2, fc_full) + bias_fc
    a = gelu(u).astype(BF)
    grad_proj = dot(a, dy, ((0,), (0,))).astype(BF)
    grad_proj_own = ring.scatter(grad_proj)
    du = (dot(after(dy, grad_proj), proj_full, ((1,), (1,))) * gelu_slope(u)).astype(BF)
    dh2_part = dot(du, fc_full, ((1,), (1,)))
    dh2 = links.scatter_seq(split(dh2_part))
    grad_fc = dot(h2, after(du, dh2_part), ((0,), (0,))).astype(BF)
    grad_fc = ring.scatter(after(grad_fc, grad_proj_own))
    dx2 = dy_wide + norm_input_grad(unit2, scale2, gain2, dh2)
    dz = dx2.astype(BF)

    do_own = jnp.pad(ring.outward(dot(dz, out_full, ((1,), (1,))).astype(BF)), ((0, 0), (0, own * size * HD - width)))
    do_blocks = [jnp.pad(do_own[:, b * own * HD : (b + 1) * own * HD], ((0, 0), (0, own % 2 * HD))) for b in range(size)]
    do_heads = jnp.concatenate(links.exchange_seq(links.relative(do_blocks)), axis=0)
    grad_out = dot(o_own, after(dz, do_own), ((0,), (0,))).astype(BF)
    output_part = dot(after(a, do_own), proj_full)
    if aligned:
        grad_out = grad_out.reshape(dps, unit_rows, width)
        blocks = [lax.dynamic_slice_in_dim(grad_out, starts[j], window, 1) for j in range(size)]
    else:
        grad_out = grad_out.reshape(dps, size, -1)
        blocks = [lax.dynamic_index_in_dim(grad_out, rank ^ j, 1, keepdims=False) for j in range(size)]
    do_heads = after(do_heads, output_part, *blocks, grad_proj_own)
    dmixed = attention_backward(info, mixed, do_heads, own, size)
    grad_out = after(links.scatter_seq(blocks).astype(BF), grad_fc)
    if aligned:
        grad_out = ring.outward(ring.scatter(grad_out.reshape(-1, width)))
        grad_out = lax.dynamic_slice_in_dim(grad_out, rows * rank - starts[0], rows, 0)
    else:
        grad_out = lax.psum_scatter(grad_out, "dp", scatter_dimension=0, tiled=True).astype(F32)
    grad_qkv = dot(h1, after(dmixed, grad_fc), ((0,), (0,))).astype(BF)
    grad_qkv_own = ring.scatter(grad_qkv)
    dh1_part = dot(after(dmixed, grad_qkv), qkv_full, ((1,), (1,)))
    output = ring.outward((x2 + links.scatter_seq(split(output_part)) + bias_p).astype(BF))
    dh1 = links.scatter_seq(split(dh1_part))
    fc_rows = links.rows_from_columns(grad_fc, unpack_fc)
    behind = links.shift(fc_rows[:tail], -1)
    unit1, scale1 = normal(x_own.astype(F32))
    input_grad = ring.outward(dx2 + norm_input_grad(unit1, scale1, gain1, dh1))

    total = lambda m: jnp.sum(m.astype(F32), axis=0)
    own_sum = lambda m: ring.outward(total(m))
    place_cols = lambda v, unpack: unpack([jnp.where(rank == b, v, 0.0)[None] for b in range(size)])[0]
    wide = place_cols(total(dmixed), lambda p: unpack_heads(p, width)).reshape(3, width)
    wide_bf = place_cols(total(du), unpack_fc)
    sums = jnp.concatenate([
        own_sum(dh1_part * unit1_all), own_sum(dh1_part), wide[0], wide[2],
        own_sum(dz), own_sum(dh2 * unit2), own_sum(dh2), own_sum(dy_wide), wide_bf,
    ])
    sums = links.all_sum(sums, ("seq", "dp"))
    vec1 = lax.dynamic_slice_in_dim(sums[: 4 * width], device * part, part)
    vec2 = lax.dynamic_slice_in_dim(sums[4 * width : 8 * width], device * part, part)
    sum_bf = sums[8 * width :]

    qkv_flat = links.rows_from_columns(grad_qkv_own, lambda p: unpack_heads(p, width)).astype(F32)
    behind = jnp.where(last, jnp.pad(sum_bf, (0, tail - hidden)), behind.astype(F32))
    fc_flat_grad = lax.dynamic_slice_in_dim(
        jnp.concatenate([fc_rows.astype(F32), behind]), shift * device, w_fc.shape[0]
    )
    return (output[None], input_grad[None], qkv_flat, grad_out.reshape(-1), fc_flat_grad, ring.outward(grad_proj_own).reshape(-1), vec1, vec2)


def solution(mesh):
    tokens = P("dp", "seq", None)
    flat = P(("dp", "seq"))
    return jax.shard_map(
        partial(local, mesh.shape["seq"], mesh.shape["dp"]),
        mesh=mesh,
        in_specs=(tokens, tokens, P("dp"), *[flat] * 6),
        out_specs=(tokens, tokens, *[flat] * 6),
        check_vma=False,
    )
```

```python
from functools import partial

import jax
import jax.numpy as jnp
from jax import lax
from jax.experimental import pallas as pl
from jax.experimental.pallas import tpu as pltpu
from jax.sharding import PartitionSpec as P

HD = 64
EPS = 1e-05
LANES = 128
BF = jnp.bfloat16
F32 = jnp.float32


def bits_of(size):
    return [1 << k for k in reversed(range(size.bit_length() - 1))]


def after(value, *others):
    others = [o for o in others if o is not None]
    return lax.optimization_barrier((value, *others))[0] if others else value


def pick(pieces, index):
    out = pieces[0]
    for k in range(1, len(pieces)):
        out = jnp.where(index == k, pieces[k], out)
    return out


class Links:
    def __init__(self, dps, seqs):
        self.sizes = {"dp": dps, "seq": seqs}
        self.last = {}

    def ordered(self, value, link, permute):
        self.last[link] = permute(after(value, self.last.get(link)))
        return self.last[link]

    def swap(self, value, axis, bits, free=False):
        pairs = [(i, i ^ bits) for i in range(self.sizes[axis])]
        if free:
            return lax.ppermute(value, axis, pairs)
        top = 1 << (bits.bit_length() - 1)
        return self.ordered(value, (axis, top), lambda v: lax.ppermute(v, axis, pairs))

    def shift(self, value, step):
        count = self.sizes["dp"] * self.sizes["seq"]
        pairs = [(i, i + step) for i in range(count) if 0 <= i + step < count]
        return self.ordered(value, ("seq", 1), lambda v: lax.ppermute(v, ("dp", "seq"), pairs))

    def all_sum(self, value, axes, free=False):
        for axis in axes:
            for bit in bits_of(self.sizes[axis]):
                value = value + self.swap(value, axis, bit, free)
        return value

    def gather_seq(self, value, free=False):
        pieces = {0: value}
        for bit in bits_of(self.sizes["seq"]):
            for j in list(pieces):
                pieces[j ^ bit] = self.swap(pieces[j], "seq", bit, free)
        return [pieces[j] for j in range(len(pieces))]

    def scatter_seq(self, blocks, last=None, free=False):
        blocks = dict(enumerate(blocks))
        for bit in reversed(bits_of(self.sizes["seq"])):
            for j in sorted(blocks, reverse=True):
                if j & bit:
                    got = after(self.swap(blocks.pop(j).astype(BF), "seq", bit, free), last if j == bit and j > 1 else None)
                    blocks[j ^ bit] = blocks[j ^ bit].astype(F32) + got.astype(F32)
        return blocks[0]

    def exchange_seq(self, pieces):
        return [pieces[0]] + [self.swap(pieces[j], "seq", j, True) for j in range(1, len(pieces))]

    def relative(self, pieces, axis="seq"):
        mine, size = lax.axis_index(axis), len(pieces)
        return [pick([pieces[j ^ m] for m in range(size)], mine) for j in range(size)]

    def columns_from_rows(self, flats, rows, columns):
        size, rank = self.sizes["seq"], lax.axis_index("seq")
        shape = lambda flat: (-1, flat.shape[0] * size // rows)
        own = sum(count for _, _, count in columns(0))
        if rows % size == 0:
            part = rows // size
            plans = [[in_columns(columns(q ^ j), part) for j in range(size)] for q in range(size)]
            pieces = rearrange([flat.reshape(shape(flat)) for flat in flats], [(part, own)] * size, plans, rank)
            return jnp.concatenate(self.relative(self.exchange_seq(pieces)), axis=0)
        full = [lax.all_gather(flat, "seq", axis=0, tiled=True).reshape(shape(flat)) for flat in flats]
        return rearrange(full, [(rows, own)], [[in_columns(columns(q), rows)] for q in range(size)], rank)[0]

    def rows_from_columns(self, value, widths, columns):
        size, rank = self.sizes["seq"], lax.axis_index("seq")
        rows = value.shape[0]
        value = value.astype(BF)
        if rows % size == 0:
            part = rows // size
            pieces = self.relative([value[b * part : (b + 1) * part] for b in range(size)])
            plans = [from_columns([columns(q ^ j) for j in range(size)], part, len(widths)) for q in range(size)]
            out = rearrange(self.exchange_seq(pieces), [(part, w) for w in widths], plans, rank, F32)
            return [matrix.reshape(-1) for matrix in out]
        full = lax.all_gather(value, "seq", axis=0, tiled=False)
        plans = [from_columns([columns(b) for b in range(size)], rows, len(widths))]
        out = []
        for matrix in rearrange([full[b] for b in range(size)], [(rows, w) for w in widths], plans, dtype=F32):
            count = matrix.size // size
            out.append(lax.dynamic_slice_in_dim(matrix.reshape(-1), rank * count, count))
        return out


def in_columns(columns, rows):
    copies, place = [], 0
    for matrix, first, count in columns:
        copies.append((matrix, first, place, rows, count))
        place += count
    return copies


def from_columns(columns_of, rows, matrices):
    out = [[] for _ in range(matrices)]
    for which, columns in enumerate(columns_of):
        place = 0
        for matrix, first, count in columns:
            if matrix is not None:
                out[matrix].append((which, place, first, rows, count))
            place += count
    return out


def rearrange_kernel(plans, count, info, *refs):
    inputs, outputs = refs[:count], refs[count:]

    def run(plan):
        for out, copies in zip(outputs, plan):
            for which, first, place, rows, columns in copies:
                if which is None:
                    value = jnp.zeros((rows, columns), out.dtype)
                else:
                    value = inputs[which][:rows, first : first + columns].astype(out.dtype)
                out[:rows, place : place + columns] = value

    if len(plans) == 1:
        run(plans[0])
        return
    for rank, plan in enumerate(plans):
        pl.when(info[0] == rank)(partial(run, plan))


def rearrange(inputs, shapes, plans, rank=0, dtype=None):
    dtype = dtype or inputs[0].dtype
    spec = lambda shape: pl.BlockSpec(shape, lambda i, info: (0, 0))
    return pl.pallas_call(
        partial(rearrange_kernel, plans, len(inputs)),
        out_shape=[jax.ShapeDtypeStruct(shape, dtype) for shape in shapes],
        grid_spec=pltpu.PrefetchScalarGridSpec(
            num_scalar_prefetch=1,
            grid=(1,),
            in_specs=[spec(value.shape) for value in inputs],
            out_specs=[spec(shape) for shape in shapes],
        ),
        compiler_params=pltpu.CompilerParams(vmem_limit_bytes=40 << 20),
        cost_estimate=pl.CostEstimate(
            flops=0, transcendentals=0, bytes_accessed=2 * sum(value.size * value.dtype.itemsize for value in inputs)
        ),
        name="rearrange",
    )(jnp.asarray(rank, jnp.int32).reshape(1), *inputs)


class Ring:
    def __init__(self, size):
        self.size = size
        self.order = [*range(0, size, 2), *range(size - 1, 0, -2)] if size == 8 else list(range(size))
        self.groups = [self.order] if size == 8 else None

    def gather(self, value):
        return lax.all_gather(value, "dp", axis=0, tiled=True, axis_index_groups=self.groups)

    def scatter(self, value):
        total = lax.psum_scatter(value, "dp", scatter_dimension=0, tiled=True, axis_index_groups=self.groups)
        return lax.optimization_barrier(total).astype(F32)

    def inward(self, value, small=False):
        return self.blocks(value, self.order, small)

    def outward(self, value, small=False):
        return self.blocks(value, [self.order.index(d) for d in range(self.size)], small)

    def blocks(self, value, order, small):
        if self.groups is None:
            return value
        rows, width = value.shape
        part = width // self.size
        if small:
            plan = [(0, d * part, k * part, rows, part) for k, d in enumerate(order)]
            return rearrange([value], [value.shape], [[plan]])[0]
        return jnp.concatenate([value[:, d * part : (d + 1) * part] for d in order], axis=1)


def head_columns(index, size, width):
    own = -(-(width // HD) // size)
    even = own - own % 2

    def heads(part, first, count):
        start = min((index * own + first) * HD, width)
        stop = min(start + count * HD, width)
        out = [(0, part * width + start, stop - start), (None, 0, count * HD - stop + start)]
        return [entry for entry in out if entry[2]]

    out = [entry for part in range(3) for entry in heads(part, 0, even)]
    if own % 2:
        out += [entry for part in range(3) for entry in heads(part, even, 1)] + [(None, 0, HD)]
    return out


def hidden_columns(index, size, order, hidden):
    part = hidden // (len(order) * size)
    return [(0, (d * size + index) * part, part) for d in order]


def feature_columns(index, size, order, width, matrix):
    own, part = width // size, width // len(order)
    out, place = [], index * own
    while place < (index + 1) * own:
        stop = min((index + 1) * own, (place // part + 1) * part)
        out.append((matrix, order[place // part] * part + place % part, stop - place))
        place = stop
    return out


def half_masks():
    lane = lax.broadcasted_iota(jnp.int32, (1, LANES), 1)
    return [lane < HD, lane >= HD]


def row_block(ref, block, rows):
    return ref[pl.ds(pl.multiple_of(block * rows, rows), rows), :]


def attention_forward_kernel(size, pairs, odd, info, q_ref, k_ref, v_ref, o_ref, k_all, v_all):
    mine, length = info[0], info[1]
    count = q_ref.shape[0] // size
    pair = pl.program_id(0)
    last = pair == pairs - 1
    for a in range(size):
        rows = pl.ds(a * count, count)
        keys = row_block(k_ref, mine ^ a, count)
        if odd:
            keys = jnp.where(last, jnp.roll(keys, HD, axis=1), keys)
        k_all[rows, :] = keys
        v_all[rows, :] = row_block(v_ref, mine ^ a, count)
    halves = half_masks()
    zero = jnp.zeros((), BF)

    def one(a, half):
        span = (a + 1) * count
        q = jnp.where(half, row_block(q_ref, mine ^ a, count), zero)
        s = lax.dot_general(q, k_all[:span, :], (((1,), (1,)), ((), ())), preferred_element_type=F32) * 0.125
        limit = jnp.minimum(a * count + lax.broadcasted_iota(jnp.int32, (count, 1), 0), length - 1)
        allowed = lax.broadcasted_iota(jnp.int32, (count, span), 1) <= limit
        s = jnp.where(allowed, s, -1e30)
        e = jnp.exp(s - jnp.max(s, axis=1, keepdims=True))
        p = (e * (1.0 / jnp.sum(e, axis=1, keepdims=True))).astype(BF)
        return jnp.dot(p, v_all[:span, :], preferred_element_type=F32)

    for a in range(size):
        rows = pl.ds(pl.multiple_of((mine ^ a) * count, count), count)
        first = one(a, halves[0])
        if not odd:
            o_ref[rows, :] = jnp.where(halves[0], first, one(a, halves[1])).astype(BF)
            continue
        o_ref[rows, :] = jnp.where(halves[0], first, 0.0).astype(BF)

        @pl.when(jnp.logical_not(last))
        def _():
            o_ref[rows, :] = jnp.where(halves[0], o_ref[rows, :], one(a, halves[1]).astype(BF))


def attention_backward_kernel(size, pairs, odd, info, q_ref, k_ref, v_ref, g_ref, d_ref, k_all, v_all, dq, dk, dv):
    mine, length = info[0], info[1]
    count = q_ref.shape[0] // size
    pair = pl.program_id(0)
    last = pair == pairs - 1
    for a in range(size):
        rows = pl.ds(a * count, count)
        keys = row_block(k_ref, mine ^ a, count)
        if odd:
            keys = jnp.where(last, jnp.roll(keys, HD, axis=1), keys)
        k_all[rows, :] = keys
        v_all[rows, :] = row_block(v_ref, mine ^ a, count)
    dk[...] = jnp.zeros_like(dk)
    dv[...] = jnp.zeros_like(dv)
    halves = half_masks()
    zero = jnp.zeros((), BF)

    def one(a, which):
        half = halves[which]
        span = (a + 1) * count
        rows = pl.ds(a * count, count)
        q = jnp.where(half, row_block(q_ref, mine ^ a, count), zero)
        g = jnp.where(half, row_block(g_ref, mine ^ a, count), zero)
        keys, values = k_all[:span, :], v_all[:span, :]
        contract = (((1,), (1,)), ((), ()))
        s = lax.dot_general(keys, q, contract, preferred_element_type=F32) * 0.125
        limit = jnp.minimum(a * count + lax.broadcasted_iota(jnp.int32, (1, count), 1), length - 1)
        allowed = lax.broadcasted_iota(jnp.int32, (span, count), 0) <= limit
        s = jnp.where(allowed, s, -1e30)
        e = jnp.exp(s - jnp.max(s, axis=0, keepdims=True))
        p = e * (1.0 / jnp.sum(e, axis=0, keepdims=True))
        dp = lax.dot_general(values, g, contract, preferred_element_type=F32)
        inner = jnp.sum(p * dp, axis=0, keepdims=True)
        ds = (p * (dp - inner) * 0.125).astype(BF)
        dv[:span, :] += jnp.dot(p.astype(BF), g, preferred_element_type=F32)
        dk[:span, :] += jnp.dot(ds, q, preferred_element_type=F32)
        part = lax.dot_general(ds, keys, (((0,), (0,)), ((), ())), preferred_element_type=F32)
        if which == 0:
            dq[rows, :] = jnp.where(half, part, 0.0)
        else:
            dq[rows, :] = jnp.where(half, part, dq[rows, :])

    for a in range(size):
        one(a, 0)
    if odd:

        @pl.when(jnp.logical_not(last))
        def _():
            for a in range(size):
                one(a, 1)
    else:
        for a in range(size):
            one(a, 1)

    def store(block, value_of):
        cols = pl.ds(pl.multiple_of(block * LANES, LANES), LANES)
        for a in range(size):
            rows = pl.ds(pl.multiple_of((mine ^ a) * count, count), count)
            d_ref[rows, cols] = value_of(pl.ds(a * count, count)).astype(BF)

    full = pairs - 1 if odd else pairs

    def plain():
        store(pair, lambda r: dq[r, :])
        store(full + pair, lambda r: dk[r, :])
        store(2 * full + pair, lambda r: dv[r, :])

    if not odd:
        plain()
        return
    pl.when(jnp.logical_not(last))(plain)

    @pl.when(last)
    def _():
        store(3 * full, lambda r: jnp.where(halves[0], dq[r, :], jnp.roll(dk[r, :], HD, axis=1)))
        store(3 * full + 1, lambda r: jnp.where(halves[0], dv[r, :], 0.0))


def head_specs(span, pairs, odd):
    full = pairs - 1 if odd else pairs

    def spec(part):
        def index(j, info):
            if not odd:
                return (0, part * full + j)
            return (0, jnp.where(j < full, part * full + j, 3 * full + (part == 2)))

        return pl.BlockSpec((span, LANES), index)

    return [spec(0), spec(1), spec(2)]


def attention_forward(info, mixed, own, size):
    span = mixed.shape[0]
    pairs, odd = -(-own // 2), own % 2
    return pl.pallas_call(
        partial(attention_forward_kernel, size, pairs, odd),
        out_shape=jax.ShapeDtypeStruct((span, pairs * LANES), BF),
        grid_spec=pltpu.PrefetchScalarGridSpec(
            num_scalar_prefetch=1,
            grid=(pairs,),
            in_specs=head_specs(span, pairs, odd),
            out_specs=pl.BlockSpec((span, LANES), lambda j, info: (0, j)),
            scratch_shapes=[pltpu.VMEM((span, LANES), BF)] * 2,
        ),
        compiler_params=pltpu.CompilerParams(vmem_limit_bytes=40 << 20),
        cost_estimate=pl.CostEstimate(
            flops=own * span * span * 3400, transcendentals=0, bytes_accessed=mixed.size * 4
        ),
        name="attention_forward",
    )(info, mixed, mixed, mixed)


def attention_backward(info, mixed, grad, own, size):
    span = mixed.shape[0]
    pairs, odd = -(-own // 2), own % 2
    return pl.pallas_call(
        partial(attention_backward_kernel, size, pairs, odd),
        out_shape=jax.ShapeDtypeStruct(mixed.shape, BF),
        grid_spec=pltpu.PrefetchScalarGridSpec(
            num_scalar_prefetch=1,
            grid=(pairs,),
            in_specs=[*head_specs(span, pairs, odd), pl.BlockSpec((span, LANES), lambda j, info: (0, j))],
            out_specs=pl.BlockSpec(mixed.shape, lambda j, info: (0, 0)),
            scratch_shapes=[pltpu.VMEM((span, LANES), BF)] * 2 + [pltpu.VMEM((span, LANES), F32)] * 3,
        ),
        compiler_params=pltpu.CompilerParams(vmem_limit_bytes=48 << 20),
        cost_estimate=pl.CostEstimate(
            flops=own * span * span * 3400, transcendentals=0, bytes_accessed=mixed.size * 6
        ),
        name="attention_backward",
    )(info, mixed, mixed, mixed, grad)


def normal(value):
    centre = value - jnp.mean(value, axis=-1, keepdims=True)
    scale = lax.rsqrt(jnp.mean(centre * centre, axis=-1, keepdims=True) + EPS)
    return centre * scale, scale


def norm_input_grad(unit, scale, gain, grad):
    scaled = grad * gain
    return scale * (
        scaled
        - jnp.mean(scaled, axis=-1, keepdims=True)
        - unit * jnp.mean(scaled * unit, axis=-1, keepdims=True)
    )


ROOT = 0.7978845608028654
CUBIC = 0.044715


def gelu_and_slope(u):
    t = jnp.tanh(ROOT * (u + CUBIC * u * u * u))
    half = 0.5 * (1.0 + t)
    return u * half, half + 0.5 * u * (1.0 - t * t) * ROOT * (1.0 + 3.0 * CUBIC * u * u)


def dot(a, b, dims=((1,), (0,))):
    return lax.dot_general(a, b, (dims, ((), ())), preferred_element_type=F32)


def local(size, dps, tokens, cotangent, lengths, w_qkv, w_out, w_fc, w_proj, attention_vectors, block_vectors):
    _, count, width = tokens.shape
    heads = width // HD
    own = -(-heads // size)
    hidden = w_proj.shape[0] * dps * size // width
    rank = lax.axis_index("seq")
    row = lax.axis_index("dp")
    device = row * size + rank
    devices = dps * size
    length = lengths[0]
    info = jnp.stack([rank.astype(jnp.int32), length])
    unit_rows = width // dps

    links = Links(dps, size)

    ring = Ring(dps)
    quarter = width // size
    columns_qkv = lambda b: head_columns(b, size, width)
    columns_fc = lambda b: hidden_columns(b, size, ring.order, hidden)
    columns_attention = lambda b: columns_qkv(b) + feature_columns(b, size, ring.order, width, 1)

    def own_columns(value, columns):
        count = sum(entry[2] for entry in columns(0))
        plans = [[in_columns(columns(q), 1)] for q in range(size)]
        return rearrange([value.reshape(1, -1)], [(1, count)], plans, rank)[0][0]

    def all_columns(value, total, columns):
        plans = []
        for q in range(size):
            copies = from_columns([columns(q)], 1, 1)[0]
            for b in range(size):
                if b != q:
                    copies += [(None, 0, first, 1, count) for matrix, first, count in columns(b) if matrix is not None]
            plans.append([copies])
        return rearrange([value.reshape(1, -1)], [(1, total)], plans, rank)[0][0]

    split = lambda m: [m[j * count : (j + 1) * count] for j in range(size)]

    attention_part = links.columns_from_rows([w_qkv, w_out], unit_rows, columns_attention)
    attention_full = ring.gather(attention_part)
    qkv_full, out_part = attention_full[:, :-quarter], lax.optimization_barrier(attention_full[:, -quarter:])

    shift = hidden // devices
    tail = -(-shift * devices // LANES) * LANES
    before = links.shift(w_fc[-tail:], 1)
    part = attention_vectors.shape[0]
    last = device == devices - 1
    small = jnp.zeros((8 * width,), BF)
    small = lax.dynamic_update_slice_in_dim(small, attention_vectors, device * part, 0)
    small = lax.dynamic_update_slice_in_dim(small, block_vectors, 4 * width + device * part, 0)
    small = jnp.concatenate([small, jnp.where(last, w_fc[-hidden:], jnp.zeros((), BF))])
    small = links.all_sum(after(small, attention_part), ("seq", "dp")).astype(F32)
    natural = small[: 8 * width].reshape(8, width)
    gain1, shift1, _, _, bias_o, gain2, shift2, bias_p = ring.inward(natural, small=True)
    bias_fc = own_columns(small[8 * width :], columns_fc)
    bias_qkv = own_columns(jnp.concatenate([natural[2], jnp.zeros_like(natural[2]), natural[3]]), columns_qkv)

    x_own = ring.inward(tokens[0])
    x_all = jnp.concatenate(links.gather_seq(after(x_own, attention_part)), axis=0)
    place = rank * count + jnp.arange(count)
    dy_own = ring.inward(cotangent[0]) * (place < length).astype(BF)[:, None]
    dy_wide = dy_own.astype(F32)
    dy = jnp.concatenate(links.gather_seq(after(dy_own, small, x_all)), axis=0)
    plain = w_fc.shape[0] - shift
    fc_flat = lax.dynamic_slice_in_dim(jnp.concatenate([before, after(w_fc, attention_part, dy)]), tail - shift * device, plain)
    fc_part = links.columns_from_rows([fc_flat], unit_rows, columns_fc)
    fc_full = ring.gather(fc_part)

    out_parts = links.gather_seq(out_part, free=True)

    unit1_all, _ = normal(x_all.astype(F32))
    h1 = (unit1_all * gain1 + shift1).astype(BF)
    mixed = (dot(after(h1, dy), qkv_full) + bias_qkv).astype(BF)
    proj_full = ring.gather(after(ring.inward(w_proj.reshape(-1, width), small=True), fc_part, mixed))
    o_heads = attention_forward(info, mixed, own, size)
    out_parts = [after(piece, mixed) for piece in out_parts]
    o_got = links.relative(links.exchange_seq(split(o_heads)))
    o_own = jnp.concatenate([piece[:, : own * HD] for piece in o_got], axis=1)
    o_own = ring.inward(o_own[:, :width])
    projected = links.relative([dot(o_own, piece) for piece in out_parts])
    x2 = x_own.astype(F32) + jnp.concatenate(projected, axis=1) + bias_o
    unit2, scale2 = normal(x2)
    h2 = jnp.concatenate(links.gather_seq((unit2 * gain2 + shift2).astype(BF)), axis=0)

    u = dot(h2, fc_full) + bias_fc
    a, slope = gelu_and_slope(u)
    a, slope = a.astype(BF), slope.astype(BF)
    grad_proj = dot(a, dy, ((0,), (0,))).astype(BF)
    grad_proj_own = ring.scatter(grad_proj)
    du = (dot(after(dy, grad_proj), proj_full, ((1,), (1,))) * slope.astype(F32)).astype(BF)
    dh2_part = dot(du, fc_full, ((1,), (1,)))
    dh2 = links.scatter_seq(split(dh2_part))
    grad_fc = dot(h2, after(du, dh2_part), ((0,), (0,))).astype(BF)
    output_part = dot(after(a, grad_fc), proj_full)
    dh2 = after(dh2, output_part)
    grad_fc = ring.scatter(after(grad_fc, grad_proj_own))
    dx2 = dy_wide + norm_input_grad(unit2, scale2, gain2, dh2)
    dz = dx2.astype(BF)

    dz_parts = links.relative([dz[:, b * quarter : (b + 1) * quarter] for b in range(size)])
    do_own = sum(dot(dz_part, piece, ((1,), (1,))) for dz_part, piece in zip(dz_parts, out_parts))
    do_own = jnp.pad(ring.outward(do_own.astype(BF)), ((0, 0), (0, own * size * HD - width)))
    do_blocks = [jnp.pad(do_own[:, b * own * HD : (b + 1) * own * HD], ((0, 0), (0, own % 2 * HD))) for b in range(size)]
    do_heads = jnp.concatenate(links.exchange_seq(links.relative(do_blocks)), axis=0)
    grad_out = [dot(after(o_own, do_own), dz_part, ((0,), (0,))).astype(BF) for dz_part in dz_parts]
    do_heads = after(do_heads, *grad_out, grad_proj_own)
    dmixed = attention_backward(info, mixed, do_heads, own, size)
    grad_out = links.scatter_seq(grad_out, dmixed, free=True).astype(BF)
    grad_qkv = dot(h1, after(dmixed, grad_fc), ((0,), (0,))).astype(BF)
    grad_attention = jnp.concatenate([grad_qkv, grad_out], axis=1)
    dmixed = after(dmixed, grad_attention)
    grad_attention = ring.scatter(grad_attention)
    dh1_part = dot(dmixed, qkv_full, ((1,), (1,)))
    output = ring.outward((x2 + links.scatter_seq(split(after(output_part, dmixed)), free=True) + bias_p).astype(BF))
    dh1 = links.scatter_seq(split(dh1_part))
    fc_rows = links.rows_from_columns(grad_fc, [hidden], columns_fc)[0]
    behind = links.shift(fc_rows[:tail].astype(BF), -1)
    unit1, scale1 = normal(x_own.astype(F32))
    input_grad = ring.outward(dx2 + norm_input_grad(unit1, scale1, gain1, dh1))

    total = lambda m: jnp.sum(m.astype(F32), axis=0)
    wide = all_columns(total(dmixed), 3 * width, columns_qkv)
    inner = [total(dh1_part * unit1_all), total(dh1_part), total(dz), total(dh2 * unit2), total(dh2), total(dy_wide)]
    grad_g1, grad_c1, grad_bo, grad_g2, grad_c2, grad_bp = ring.outward(jnp.stack(inner), small=True)
    sums = jnp.concatenate([
        grad_g1, grad_c1, wide[:width], wide[2 * width :], grad_bo, grad_g2, grad_c2, grad_bp,
        all_columns(total(du), hidden, columns_fc),
    ])
    sums = links.all_sum(sums, ("seq", "dp"), free=True)
    vec1 = lax.dynamic_slice_in_dim(sums[: 4 * width], device * part, part)
    vec2 = lax.dynamic_slice_in_dim(sums[4 * width : 8 * width], device * part, part)
    sum_bf = sums[8 * width :]

    behind = jnp.where(last, jnp.pad(sum_bf, (0, tail - hidden)), behind.astype(F32))
    fc_flat_grad = lax.dynamic_slice_in_dim(
        jnp.concatenate([fc_rows, behind]), shift * device, w_fc.shape[0]
    )
    grad_attention = after(grad_attention, input_grad, fc_flat_grad, vec1, vec2, output)
    qkv_flat, out_flat = links.rows_from_columns(grad_attention, [3 * width, width], columns_attention)
    return (output[None], input_grad[None], qkv_flat, out_flat, fc_flat_grad, ring.outward(grad_proj_own, small=True).reshape(-1), vec1, vec2)


def solution(mesh):
    tokens = P("dp", "seq", None)
    flat = P(("dp", "seq"))
    return jax.shard_map(
        partial(local, mesh.shape["seq"], mesh.shape["dp"]),
        mesh=mesh,
        in_specs=(tokens, tokens, P("dp"), *[flat] * 6),
        out_specs=(tokens, tokens, *[flat] * 6),
        check_vma=False,
    )
```

```python
from functools import partial

import jax
import jax.numpy as jnp
from jax import lax
from jax.experimental import pallas as pl
from jax.experimental.pallas import tpu as pltpu
from jax.sharding import PartitionSpec as P

HD = 64
EPS = 1e-05
LANES = 128
BF = jnp.bfloat16
F32 = jnp.float32


def bits_of(size):
    return [1 << k for k in reversed(range(size.bit_length() - 1))]


def after(value, *others):
    others = [o for o in others if o is not None]
    return lax.optimization_barrier((value, *others))[0] if others else value


def pick(pieces, index):
    out = pieces[0]
    for k in range(1, len(pieces)):
        out = jnp.where(index == k, pieces[k], out)
    return out


class Links:
    def __init__(self, dps, seqs):
        self.sizes = {"dp": dps, "seq": seqs}
        self.last = {}
        self.sent = []

    def ordered(self, value, link, permute):
        self.last[link] = permute(after(value, self.last.get(link)))
        return self.last[link]

    def swap(self, value, axis, bits, free=False):
        pairs = [(i, i ^ bits) for i in range(self.sizes[axis])]
        if free:
            return lax.ppermute(value, axis, pairs)
        top = 1 << (bits.bit_length() - 1)
        return self.ordered(value, (axis, top), lambda v: lax.ppermute(v, axis, pairs))

    def shift(self, value, step):
        count = self.sizes["dp"] * self.sizes["seq"]
        pairs = [(i, i + step) for i in range(count) if 0 <= i + step < count]
        return self.ordered(value, ("seq", 1), lambda v: lax.ppermute(v, ("dp", "seq"), pairs))

    def all_sum(self, value, axes, free=False):
        for axis in axes:
            for bit in bits_of(self.sizes[axis]):
                value = value + self.swap(value, axis, bit, free)
        return value

    def gather_seq(self, value, free=False):
        pieces = {0: value}
        for bit in bits_of(self.sizes["seq"]):
            for j in list(pieces):
                pieces[j ^ bit] = self.swap(pieces[j], "seq", bit, free)
        return [pieces[j] for j in range(len(pieces))]

    def scatter_seq(self, blocks, last=None, free=False, hold=None):
        blocks = dict(enumerate(blocks))
        for bit in reversed(bits_of(self.sizes["seq"])):
            for j in sorted(blocks, reverse=True):
                if j & bit:
                    final = j == bit and j > 1
                    sent = after(blocks.pop(j).astype(BF), hold if final else None)
                    got = after(self.swap(sent, "seq", bit, free), last if final else None)
                    blocks[j ^ bit] = blocks[j ^ bit].astype(F32) + got.astype(F32)
        return blocks[0]

    def exchange_seq(self, pieces):
        return [pieces[0]] + [self.swap(pieces[j], "seq", j, True) for j in range(1, len(pieces))]

    def relative(self, pieces, axis="seq"):
        mine, size = lax.axis_index(axis), len(pieces)
        return [pick([pieces[j ^ m] for m in range(size)], mine) for j in range(size)]

    def columns_from_rows(self, flats, rows, columns):
        size, rank = self.sizes["seq"], lax.axis_index("seq")
        shape = lambda flat: (-1, flat.shape[0] * size // rows)
        own = sum(count for _, _, count in columns(0))
        if rows % size == 0:
            part = rows // size
            plans = [[in_columns(columns(q ^ j), part) for j in range(size)] for q in range(size)]
            pieces = rearrange([flat.reshape(shape(flat)) for flat in flats], [(part, own)] * size, plans, rank)
            return jnp.concatenate(self.relative(self.exchange_seq(pieces)), axis=0)
        full = [lax.all_gather(flat, "seq", axis=0, tiled=True).reshape(shape(flat)) for flat in flats]
        return rearrange(full, [(rows, own)], [[in_columns(columns(q), rows)] for q in range(size)], rank)[0]

    def rows_from_columns(self, value, widths, columns):
        size, rank = self.sizes["seq"], lax.axis_index("seq")
        rows = value.shape[0]
        value = value.astype(BF)
        if rows % size == 0:
            part = rows // size
            pieces = self.relative([value[b * part : (b + 1) * part] for b in range(size)])
            self.sent = pieces
            plans = [from_columns([columns(q ^ j) for j in range(size)], part, len(widths)) for q in range(size)]
            out = rearrange(self.exchange_seq(pieces), [(part, w) for w in widths], plans, rank, F32)
            return [matrix.reshape(-1) for matrix in out]
        full = lax.all_gather(value, "seq", axis=0, tiled=False)
        plans = [from_columns([columns(b) for b in range(size)], rows, len(widths))]
        out = []
        for matrix in rearrange([full[b] for b in range(size)], [(rows, w) for w in widths], plans, dtype=F32):
            count = matrix.size // size
            out.append(lax.dynamic_slice_in_dim(matrix.reshape(-1), rank * count, count))
        return out


def in_columns(columns, rows):
    copies, place = [], 0
    for matrix, first, count in columns:
        copies.append((matrix, first, place, rows, count))
        place += count
    return copies


def from_columns(columns_of, rows, matrices):
    out = [[] for _ in range(matrices)]
    for which, columns in enumerate(columns_of):
        place = 0
        for matrix, first, count in columns:
            if matrix is not None:
                out[matrix].append((which, place, first, rows, count))
            place += count
    return out


def rearrange_kernel(plans, count, info, *refs):
    inputs, outputs = refs[:count], refs[count:]

    def run(plan):
        for out, copies in zip(outputs, plan):
            for which, first, place, rows, columns in copies:
                if which is None:
                    value = jnp.zeros((rows, columns), out.dtype)
                else:
                    value = inputs[which][:rows, first : first + columns].astype(out.dtype)
                out[:rows, place : place + columns] = value

    if len(plans) == 1:
        run(plans[0])
        return
    for rank, plan in enumerate(plans):
        pl.when(info[0] == rank)(partial(run, plan))


def rearrange(inputs, shapes, plans, rank=0, dtype=None):
    dtype = dtype or inputs[0].dtype
    spec = lambda shape: pl.BlockSpec(shape, lambda i, info: (0, 0))
    return pl.pallas_call(
        partial(rearrange_kernel, plans, len(inputs)),
        out_shape=[jax.ShapeDtypeStruct(shape, dtype) for shape in shapes],
        grid_spec=pltpu.PrefetchScalarGridSpec(
            num_scalar_prefetch=1,
            grid=(1,),
            in_specs=[spec(value.shape) for value in inputs],
            out_specs=[spec(shape) for shape in shapes],
        ),
        compiler_params=pltpu.CompilerParams(vmem_limit_bytes=40 << 20),
        cost_estimate=pl.CostEstimate(
            flops=0, transcendentals=0, bytes_accessed=2 * sum(value.size * value.dtype.itemsize for value in inputs)
        ),
        name="rearrange",
    )(jnp.asarray(rank, jnp.int32).reshape(1), *inputs)


class Ring:
    def __init__(self, size):
        self.size = size
        self.order = [*range(0, size, 2), *range(size - 1, 0, -2)] if size == 8 else list(range(size))
        self.groups = [self.order] if size == 8 else None

    def gather(self, value):
        return lax.all_gather(value, "dp", axis=0, tiled=True, axis_index_groups=self.groups)

    def scatter(self, value):
        total = lax.psum_scatter(value, "dp", scatter_dimension=0, tiled=True, axis_index_groups=self.groups)
        return lax.optimization_barrier(total).astype(F32)

    def inward(self, value, small=False):
        return self.blocks(value, self.order, small)

    def outward(self, value, small=False):
        return self.blocks(value, [self.order.index(d) for d in range(self.size)], small)

    def blocks(self, value, order, small):
        if self.groups is None:
            return value
        rows, width = value.shape
        part = width // self.size
        if small:
            plan = [(0, d * part, k * part, rows, part) for k, d in enumerate(order)]
            return rearrange([value], [value.shape], [[plan]])[0]
        return jnp.concatenate([value[:, d * part : (d + 1) * part] for d in order], axis=1)


def head_columns(index, size, width):
    own = -(-(width // HD) // size)
    even = own - own % 2

    def heads(part, first, count):
        start = min((index * own + first) * HD, width)
        stop = min(start + count * HD, width)
        out = [(0, part * width + start, stop - start), (None, 0, count * HD - stop + start)]
        return [entry for entry in out if entry[2]]

    out = [entry for part in range(3) for entry in heads(part, 0, even)]
    if own % 2:
        out += [entry for part in range(3) for entry in heads(part, even, 1)] + [(None, 0, HD)]
    return out


def hidden_columns(index, size, order, hidden):
    part = hidden // (len(order) * size)
    return [(0, (d * size + index) * part, part) for d in order]


def feature_columns(index, size, order, width, matrix):
    own, part = width // size, width // len(order)
    out, place = [], index * own
    while place < (index + 1) * own:
        stop = min((index + 1) * own, (place // part + 1) * part)
        out.append((matrix, order[place // part] * part + place % part, stop - place))
        place = stop
    return out


def half_masks():
    lane = lax.broadcasted_iota(jnp.int32, (1, LANES), 1)
    return [lane < HD, lane >= HD]


def row_block(ref, block, rows):
    return ref[pl.ds(pl.multiple_of(block * rows, rows), rows), :]


def attention_forward_kernel(size, pairs, odd, info, q_ref, k_ref, v_ref, o_ref, k_all, v_all):
    mine, length = info[0], info[1]
    count = q_ref.shape[0] // size
    pair = pl.program_id(0)
    last = pair == pairs - 1
    for a in range(size):
        rows = pl.ds(a * count, count)
        keys = row_block(k_ref, mine ^ a, count)
        if odd:
            keys = jnp.where(last, jnp.roll(keys, HD, axis=1), keys)
        k_all[rows, :] = keys
        v_all[rows, :] = row_block(v_ref, mine ^ a, count)
    halves = half_masks()
    zero = jnp.zeros((), BF)

    def one(a, half):
        span = (a + 1) * count
        q = jnp.where(half, row_block(q_ref, mine ^ a, count), zero)
        s = lax.dot_general(q, k_all[:span, :], (((1,), (1,)), ((), ())), preferred_element_type=F32) * 0.125
        limit = jnp.minimum(a * count + lax.broadcasted_iota(jnp.int32, (count, 1), 0), length - 1)
        allowed = lax.broadcasted_iota(jnp.int32, (count, span), 1) <= limit
        s = jnp.where(allowed, s, -1e30)
        e = jnp.exp(s - jnp.max(s, axis=1, keepdims=True))
        p = (e * (1.0 / jnp.sum(e, axis=1, keepdims=True))).astype(BF)
        return jnp.dot(p, v_all[:span, :], preferred_element_type=F32)

    for a in range(size):
        rows = pl.ds(pl.multiple_of((mine ^ a) * count, count), count)
        first = one(a, halves[0])
        if not odd:
            o_ref[rows, :] = jnp.where(halves[0], first, one(a, halves[1])).astype(BF)
            continue
        o_ref[rows, :] = jnp.where(halves[0], first, 0.0).astype(BF)

        @pl.when(jnp.logical_not(last))
        def _():
            o_ref[rows, :] = jnp.where(halves[0], o_ref[rows, :], one(a, halves[1]).astype(BF))


def attention_backward_kernel(size, pairs, odd, info, q_ref, k_ref, v_ref, g_ref, d_ref, k_all, v_all, dq, dk, dv):
    mine, length = info[0], info[1]
    count = q_ref.shape[0] // size
    pair = pl.program_id(0)
    last = pair == pairs - 1
    for a in range(size):
        rows = pl.ds(a * count, count)
        keys = row_block(k_ref, mine ^ a, count)
        if odd:
            keys = jnp.where(last, jnp.roll(keys, HD, axis=1), keys)
        k_all[rows, :] = keys
        v_all[rows, :] = row_block(v_ref, mine ^ a, count)
    dk[...] = jnp.zeros_like(dk)
    dv[...] = jnp.zeros_like(dv)
    halves = half_masks()
    zero = jnp.zeros((), BF)

    def one(a, which):
        half = halves[which]
        span = (a + 1) * count
        rows = pl.ds(a * count, count)
        q = jnp.where(half, row_block(q_ref, mine ^ a, count), zero)
        g = jnp.where(half, row_block(g_ref, mine ^ a, count), zero)
        keys, values = k_all[:span, :], v_all[:span, :]
        contract = (((1,), (1,)), ((), ()))
        s = lax.dot_general(keys, q, contract, preferred_element_type=F32) * 0.125
        limit = jnp.minimum(a * count + lax.broadcasted_iota(jnp.int32, (1, count), 1), length - 1)
        allowed = lax.broadcasted_iota(jnp.int32, (span, count), 0) <= limit
        s = jnp.where(allowed, s, -1e30)
        e = jnp.exp(s - jnp.max(s, axis=0, keepdims=True))
        p = e * (1.0 / jnp.sum(e, axis=0, keepdims=True))
        dp = lax.dot_general(values, g, contract, preferred_element_type=F32)
        inner = jnp.sum(p * dp, axis=0, keepdims=True)
        ds = (p * (dp - inner) * 0.125).astype(BF)
        dv[:span, :] += jnp.dot(p.astype(BF), g, preferred_element_type=F32)
        dk[:span, :] += jnp.dot(ds, q, preferred_element_type=F32)
        part = lax.dot_general(ds, keys, (((0,), (0,)), ((), ())), preferred_element_type=F32)
        if which == 0:
            dq[rows, :] = jnp.where(half, part, 0.0)
        else:
            dq[rows, :] = jnp.where(half, part, dq[rows, :])

    for a in range(size):
        one(a, 0)
    if odd:

        @pl.when(jnp.logical_not(last))
        def _():
            for a in range(size):
                one(a, 1)
    else:
        for a in range(size):
            one(a, 1)

    def store(block, value_of):
        cols = pl.ds(pl.multiple_of(block * LANES, LANES), LANES)
        for a in range(size):
            rows = pl.ds(pl.multiple_of((mine ^ a) * count, count), count)
            d_ref[rows, cols] = value_of(pl.ds(a * count, count)).astype(BF)

    full = pairs - 1 if odd else pairs

    def plain():
        store(pair, lambda r: dq[r, :])
        store(full + pair, lambda r: dk[r, :])
        store(2 * full + pair, lambda r: dv[r, :])

    if not odd:
        plain()
        return
    pl.when(jnp.logical_not(last))(plain)

    @pl.when(last)
    def _():
        store(3 * full, lambda r: jnp.where(halves[0], dq[r, :], jnp.roll(dk[r, :], HD, axis=1)))
        store(3 * full + 1, lambda r: jnp.where(halves[0], dv[r, :], 0.0))


def head_specs(span, pairs, odd):
    full = pairs - 1 if odd else pairs

    def spec(part):
        def index(j, info):
            if not odd:
                return (0, part * full + j)
            return (0, jnp.where(j < full, part * full + j, 3 * full + (part == 2)))

        return pl.BlockSpec((span, LANES), index)

    return [spec(0), spec(1), spec(2)]


def attention_forward(info, mixed, own, size):
    span = mixed.shape[0]
    pairs, odd = -(-own // 2), own % 2
    return pl.pallas_call(
        partial(attention_forward_kernel, size, pairs, odd),
        out_shape=jax.ShapeDtypeStruct((span, pairs * LANES), BF),
        grid_spec=pltpu.PrefetchScalarGridSpec(
            num_scalar_prefetch=1,
            grid=(pairs,),
            in_specs=head_specs(span, pairs, odd),
            out_specs=pl.BlockSpec((span, LANES), lambda j, info: (0, j)),
            scratch_shapes=[pltpu.VMEM((span, LANES), BF)] * 2,
        ),
        compiler_params=pltpu.CompilerParams(vmem_limit_bytes=40 << 20),
        cost_estimate=pl.CostEstimate(
            flops=own * span * span * 3400, transcendentals=0, bytes_accessed=mixed.size * 4
        ),
        name="attention_forward",
    )(info, mixed, mixed, mixed)


def attention_backward(info, mixed, grad, own, size):
    span = mixed.shape[0]
    pairs, odd = -(-own // 2), own % 2
    return pl.pallas_call(
        partial(attention_backward_kernel, size, pairs, odd),
        out_shape=jax.ShapeDtypeStruct(mixed.shape, BF),
        grid_spec=pltpu.PrefetchScalarGridSpec(
            num_scalar_prefetch=1,
            grid=(pairs,),
            in_specs=[*head_specs(span, pairs, odd), pl.BlockSpec((span, LANES), lambda j, info: (0, j))],
            out_specs=pl.BlockSpec(mixed.shape, lambda j, info: (0, 0)),
            scratch_shapes=[pltpu.VMEM((span, LANES), BF)] * 2 + [pltpu.VMEM((span, LANES), F32)] * 3,
        ),
        compiler_params=pltpu.CompilerParams(vmem_limit_bytes=48 << 20),
        cost_estimate=pl.CostEstimate(
            flops=own * span * span * 3400, transcendentals=0, bytes_accessed=mixed.size * 6
        ),
        name="attention_backward",
    )(info, mixed, mixed, mixed, grad)


def normal(value):
    centre = value - jnp.mean(value, axis=-1, keepdims=True)
    scale = lax.rsqrt(jnp.mean(centre * centre, axis=-1, keepdims=True) + EPS)
    return centre * scale, scale


def norm_input_grad(unit, scale, gain, grad):
    scaled = grad * gain
    return scale * (
        scaled
        - jnp.mean(scaled, axis=-1, keepdims=True)
        - unit * jnp.mean(scaled * unit, axis=-1, keepdims=True)
    )


ROOT = 0.7978845608028654
CUBIC = 0.044715


def gelu_and_slope(u):
    t = jnp.tanh(ROOT * (u + CUBIC * u * u * u))
    half = 0.5 * (1.0 + t)
    return u * half, half + 0.5 * u * (1.0 - t * t) * ROOT * (1.0 + 3.0 * CUBIC * u * u)


def dot(a, b, dims=((1,), (0,))):
    return lax.dot_general(a, b, (dims, ((), ())), preferred_element_type=F32)


def local(size, dps, tokens, cotangent, lengths, w_qkv, w_out, w_fc, w_proj, attention_vectors, block_vectors):
    _, count, width = tokens.shape
    heads = width // HD
    own = -(-heads // size)
    hidden = w_proj.shape[0] * dps * size // width
    rank = lax.axis_index("seq")
    row = lax.axis_index("dp")
    device = row * size + rank
    devices = dps * size
    length = lengths[0]
    info = jnp.stack([rank.astype(jnp.int32), length])
    unit_rows = width // dps

    links = Links(dps, size)

    ring = Ring(dps)
    quarter = width // size
    columns_qkv = lambda b: head_columns(b, size, width)
    columns_fc = lambda b: hidden_columns(b, size, ring.order, hidden)
    columns_attention = lambda b: columns_qkv(b) + feature_columns(b, size, ring.order, width, 1)

    def own_columns(value, columns):
        count = sum(entry[2] for entry in columns(0))
        plans = [[in_columns(columns(q), 1)] for q in range(size)]
        return rearrange([value.reshape(1, -1)], [(1, count)], plans, rank)[0][0]

    def all_columns(value, total, columns):
        plans = []
        for q in range(size):
            copies = from_columns([columns(q)], 1, 1)[0]
            for b in range(size):
                if b != q:
                    copies += [(None, 0, first, 1, count) for matrix, first, count in columns(b) if matrix is not None]
            plans.append([copies])
        return rearrange([value.reshape(1, -1)], [(1, total)], plans, rank)[0][0]

    split = lambda m: [m[j * count : (j + 1) * count] for j in range(size)]

    attention_part = links.columns_from_rows([w_qkv, w_out], unit_rows, columns_attention)
    attention_full = ring.gather(attention_part)
    qkv_full, out_part = attention_full[:, :-quarter], lax.optimization_barrier(attention_full[:, -quarter:])

    shift = hidden // devices
    tail = -(-shift * devices // LANES) * LANES
    before = links.shift(after(w_fc[-tail:], attention_part), 1)
    part = attention_vectors.shape[0]
    last = device == devices - 1
    small = jnp.zeros((8 * width,), BF)
    small = lax.dynamic_update_slice_in_dim(small, attention_vectors, device * part, 0)
    small = lax.dynamic_update_slice_in_dim(small, block_vectors, 4 * width + device * part, 0)
    small = jnp.concatenate([small, jnp.where(last, w_fc[-hidden:], jnp.zeros((), BF))])
    small = links.all_sum(after(small, attention_part), ("seq", "dp")).astype(F32)
    natural = small[: 8 * width].reshape(8, width)
    gain1, shift1, _, _, bias_o, gain2, shift2, bias_p = ring.inward(natural, small=True)
    bias_fc = own_columns(small[8 * width :], columns_fc)
    bias_qkv = own_columns(jnp.concatenate([natural[2], jnp.zeros_like(natural[2]), natural[3]]), columns_qkv)

    x_own = ring.inward(tokens[0])
    x_all = jnp.concatenate(links.gather_seq(after(x_own, attention_part)), axis=0)
    place = rank * count + jnp.arange(count)
    dy_own = ring.inward(cotangent[0]) * (place < length).astype(BF)[:, None]
    dy_wide = dy_own.astype(F32)
    dy = jnp.concatenate(links.gather_seq(after(dy_own, small, x_all)), axis=0)
    unit1_all, _ = normal(x_all.astype(F32))
    h1 = (unit1_all * gain1 + shift1).astype(BF)
    plain = w_fc.shape[0] - shift
    fc_flat = lax.dynamic_slice_in_dim(jnp.concatenate([before, after(w_fc, attention_part, dy, h1)]), tail - shift * device, plain)
    fc_part = links.columns_from_rows([fc_flat], unit_rows, columns_fc)
    fc_full = ring.gather(fc_part)

    out_parts = links.gather_seq(out_part, free=True)

    mixed = (dot(after(h1, dy), qkv_full) + bias_qkv).astype(BF)
    proj_full = ring.gather(after(ring.inward(w_proj.reshape(-1, width), small=True), fc_part, mixed))
    o_heads = attention_forward(info, mixed, own, size)
    out_parts = [after(piece, mixed) for piece in out_parts]
    o_got = links.relative(links.exchange_seq(split(o_heads)))
    o_own = jnp.concatenate([piece[:, : own * HD] for piece in o_got], axis=1)
    o_own = ring.inward(o_own[:, :width])
    projected = links.relative([dot(o_own, piece) for piece in out_parts])
    x2 = x_own.astype(F32) + jnp.concatenate(projected, axis=1) + bias_o
    unit2, scale2 = normal(x2)
    h2 = jnp.concatenate(links.gather_seq((unit2 * gain2 + shift2).astype(BF)), axis=0)

    u = dot(h2, fc_full) + bias_fc
    a, slope = gelu_and_slope(u)
    a, slope = a.astype(BF), slope.astype(BF)
    grad_proj = dot(a, dy, ((0,), (0,))).astype(BF)
    grad_proj_own = ring.scatter(grad_proj)
    du = (dot(after(dy, grad_proj), proj_full, ((1,), (1,))) * slope.astype(F32)).astype(BF)
    dh2_part = dot(du, fc_full, ((1,), (1,)))
    dh2 = links.scatter_seq(split(dh2_part))
    grad_fc = dot(h2, after(du, dh2_part), ((0,), (0,))).astype(BF)
    output_part = dot(after(a, grad_fc), proj_full)
    dh2 = after(dh2, output_part)
    grad_fc = ring.scatter(after(grad_fc, grad_proj_own))
    dx2 = dy_wide + norm_input_grad(unit2, scale2, gain2, dh2)
    dz = dx2.astype(BF)

    dz_parts = links.relative([dz[:, b * quarter : (b + 1) * quarter] for b in range(size)])
    do_own = sum(dot(dz_part, piece, ((1,), (1,))) for dz_part, piece in zip(dz_parts, out_parts))
    do_own = jnp.pad(ring.outward(do_own.astype(BF)), ((0, 0), (0, own * size * HD - width)))
    do_blocks = [jnp.pad(do_own[:, b * own * HD : (b + 1) * own * HD], ((0, 0), (0, own % 2 * HD))) for b in range(size)]
    do_heads = jnp.concatenate(links.exchange_seq(links.relative(do_blocks)), axis=0)
    grad_out = [dot(after(o_own, do_own), dz_part, ((0,), (0,))).astype(BF) for dz_part in dz_parts]
    do_heads = after(do_heads, *grad_out, grad_proj_own)
    dmixed = attention_backward(info, mixed, do_heads, own, size)
    grad_out = links.scatter_seq(grad_out, dmixed, free=True).astype(BF)
    dh1_part = dot(dmixed, qkv_full, ((1,), (1,)))
    grad_qkv = dot(h1, after(dmixed, dh1_part), ((0,), (0,))).astype(BF)
    grad_attention = jnp.concatenate([grad_qkv, grad_out], axis=1)
    dh1_part, dmixed, grad_fc = (after(value, grad_attention) for value in (dh1_part, dmixed, grad_fc))
    output = links.scatter_seq(split(output_part), free=True, hold=grad_attention)
    output = ring.outward((x2 + output + bias_p).astype(BF))
    grad_attention = ring.scatter(grad_attention)
    fc_rows = links.rows_from_columns(grad_fc, [hidden], columns_fc)[0]
    behind = links.shift(fc_rows[:tail].astype(BF), -1)
    total = lambda m: jnp.sum(m.astype(F32), axis=0)
    wide = all_columns(total(dmixed), 3 * width, columns_qkv)
    inner = [total(dh1_part * unit1_all), total(dh1_part), total(dz), total(dh2 * unit2), total(dh2), total(dy_wide)]
    grad_g1, grad_c1, grad_bo, grad_g2, grad_c2, grad_bp = ring.outward(jnp.stack(inner), small=True)
    sums = jnp.concatenate([
        grad_g1, grad_c1, wide[:width], wide[2 * width :], grad_bo, grad_g2, grad_c2, grad_bp,
        all_columns(total(du), hidden, columns_fc),
    ])
    sums = links.all_sum(sums, ("seq",), free=True)
    dh1 = links.scatter_seq(split(dh1_part), free=True, hold=sums)
    qkv_flat, out_flat = links.rows_from_columns(grad_attention, [3 * width, width], columns_attention)
    dh1 = after(dh1, *links.sent)
    unit1, scale1 = normal(x_own.astype(F32))
    input_grad = ring.outward(dx2 + norm_input_grad(unit1, scale1, gain1, dh1))

    sums = links.all_sum(sums, ("dp",), free=True)
    vec1 = lax.dynamic_slice_in_dim(sums[: 4 * width], device * part, part)
    vec2 = lax.dynamic_slice_in_dim(sums[4 * width : 8 * width], device * part, part)
    sum_bf = sums[8 * width :]

    behind = jnp.where(last, jnp.pad(sum_bf, (0, tail - hidden)), behind.astype(F32))
    fc_flat_grad = lax.dynamic_slice_in_dim(
        jnp.concatenate([fc_rows, behind]), shift * device, w_fc.shape[0]
    )
    grad_attention = after(grad_attention, input_grad, fc_flat_grad, vec1, vec2, output)
    return (output[None], input_grad[None], qkv_flat, out_flat, fc_flat_grad, ring.outward(grad_proj_own, small=True).reshape(-1), vec1, vec2)


def solution(mesh):
    tokens = P("dp", "seq", None)
    flat = P(("dp", "seq"))
    return jax.shard_map(
        partial(local, mesh.shape["seq"], mesh.shape["dp"]),
        mesh=mesh,
        in_specs=(tokens, tokens, P("dp"), *[flat] * 6),
        out_specs=(tokens, tokens, *[flat] * 6),
        check_vma=False,
    )
```

```python
from functools import partial

import jax
import jax.numpy as jnp
from jax import lax
from jax.experimental import pallas as pl
from jax.experimental.pallas import tpu as pltpu
from jax.sharding import PartitionSpec as P

HD = 64
EPS = 1e-05
LANES = 128
BF = jnp.bfloat16
F32 = jnp.float32


def bits_of(size):
    return [1 << k for k in reversed(range(size.bit_length() - 1))]


def after(value, *others):
    others = [o for o in others if o is not None]
    return lax.optimization_barrier((value, *others))[0] if others else value


def pick(pieces, index):
    out = pieces[0]
    for k in range(1, len(pieces)):
        out = jnp.where(index == k, pieces[k], out)
    return out


class Links:
    def __init__(self, dps, seqs):
        self.sizes = {"dp": dps, "seq": seqs}
        self.last = {}
        self.sent = []

    def ordered(self, value, link, permute):
        self.last[link] = permute(after(value, self.last.get(link)))
        return self.last[link]

    def swap(self, value, axis, bits, free=False):
        pairs = [(i, i ^ bits) for i in range(self.sizes[axis])]
        if free:
            return lax.ppermute(value, axis, pairs)
        top = 1 << (bits.bit_length() - 1)
        return self.ordered(value, (axis, top), lambda v: lax.ppermute(v, axis, pairs))

    def shift(self, value, step):
        count = self.sizes["dp"] * self.sizes["seq"]
        pairs = [(i, i + step) for i in range(count) if 0 <= i + step < count]
        return self.ordered(value, ("seq", 1), lambda v: lax.ppermute(v, ("dp", "seq"), pairs))

    def all_sum(self, value, axes, free=False):
        for axis in axes:
            for bit in bits_of(self.sizes[axis]):
                value = value + self.swap(value, axis, bit, free)
        return value

    def gather_seq(self, value, free=False):
        pieces = {0: value}
        for bit in bits_of(self.sizes["seq"]):
            for j in list(pieces):
                pieces[j ^ bit] = self.swap(pieces[j], "seq", bit, free)
        return [pieces[j] for j in range(len(pieces))]

    def scatter_seq(self, blocks, last=None, free=False, hold=None):
        blocks = dict(enumerate(blocks))
        for bit in reversed(bits_of(self.sizes["seq"])):
            for j in sorted(blocks, reverse=True):
                if j & bit:
                    final = j == bit and j > 1
                    sent = after(blocks.pop(j).astype(BF), hold if final else None)
                    got = after(self.swap(sent, "seq", bit, free), last if final else None)
                    blocks[j ^ bit] = blocks[j ^ bit].astype(F32) + got.astype(F32)
        return blocks[0]

    def exchange_seq(self, pieces):
        return [pieces[0]] + [self.swap(pieces[j], "seq", j, True) for j in range(1, len(pieces))]

    def relative(self, pieces, axis="seq"):
        mine, size = lax.axis_index(axis), len(pieces)
        return [pick([pieces[j ^ m] for m in range(size)], mine) for j in range(size)]

    def columns_from_rows(self, flats, rows, columns):
        size, rank = self.sizes["seq"], lax.axis_index("seq")
        shape = lambda flat: (-1, flat.shape[0] * size // rows)
        own = sum(count for _, _, count in columns(0))
        if rows % size == 0:
            part = rows // size
            plans = [[in_columns(columns(q ^ j), part) for j in range(size)] for q in range(size)]
            pieces = rearrange([flat.reshape(shape(flat)) for flat in flats], [(part, own)] * size, plans, rank)
            return jnp.concatenate(self.relative(self.exchange_seq(pieces)), axis=0)
        full = [lax.all_gather(flat, "seq", axis=0, tiled=True).reshape(shape(flat)) for flat in flats]
        return rearrange(full, [(rows, own)], [[in_columns(columns(q), rows)] for q in range(size)], rank)[0]

    def rows_from_columns(self, value, widths, columns):
        size, rank = self.sizes["seq"], lax.axis_index("seq")
        rows = value.shape[0]
        value = value.astype(BF)
        if rows % size == 0:
            part = rows // size
            pieces = self.relative([value[b * part : (b + 1) * part] for b in range(size)])
            self.sent = pieces
            plans = [from_columns([columns(q ^ j) for j in range(size)], part, len(widths)) for q in range(size)]
            out = rearrange(self.exchange_seq(pieces), [(part, w) for w in widths], plans, rank, F32)
            return [matrix.reshape(-1) for matrix in out]
        full = lax.all_gather(value, "seq", axis=0, tiled=False)
        plans = [from_columns([columns(b) for b in range(size)], rows, len(widths))]
        out = []
        for matrix in rearrange([full[b] for b in range(size)], [(rows, w) for w in widths], plans, dtype=F32):
            count = matrix.size // size
            out.append(lax.dynamic_slice_in_dim(matrix.reshape(-1), rank * count, count))
        return out


def in_columns(columns, rows):
    copies, place = [], 0
    for matrix, first, count in columns:
        copies.append((matrix, first, place, rows, count))
        place += count
    return copies


def from_columns(columns_of, rows, matrices):
    out = [[] for _ in range(matrices)]
    for which, columns in enumerate(columns_of):
        place = 0
        for matrix, first, count in columns:
            if matrix is not None:
                out[matrix].append((which, place, first, rows, count))
            place += count
    return out


def rearrange_kernel(plans, count, info, *refs):
    inputs, outputs = refs[:count], refs[count:]

    def run(plan):
        for out, copies in zip(outputs, plan):
            for which, first, place, rows, columns in copies:
                if which is None:
                    value = jnp.zeros((rows, columns), out.dtype)
                else:
                    value = inputs[which][:rows, first : first + columns].astype(out.dtype)
                out[:rows, place : place + columns] = value

    if len(plans) == 1:
        run(plans[0])
        return
    for rank, plan in enumerate(plans):
        pl.when(info[0] == rank)(partial(run, plan))


def rearrange(inputs, shapes, plans, rank=0, dtype=None):
    dtype = dtype or inputs[0].dtype
    spec = lambda shape: pl.BlockSpec(shape, lambda i, info: (0, 0))
    return pl.pallas_call(
        partial(rearrange_kernel, plans, len(inputs)),
        out_shape=[jax.ShapeDtypeStruct(shape, dtype) for shape in shapes],
        grid_spec=pltpu.PrefetchScalarGridSpec(
            num_scalar_prefetch=1,
            grid=(1,),
            in_specs=[spec(value.shape) for value in inputs],
            out_specs=[spec(shape) for shape in shapes],
        ),
        compiler_params=pltpu.CompilerParams(vmem_limit_bytes=40 << 20),
        cost_estimate=pl.CostEstimate(
            flops=0, transcendentals=0, bytes_accessed=2 * sum(value.size * value.dtype.itemsize for value in inputs)
        ),
        name="rearrange",
    )(jnp.asarray(rank, jnp.int32).reshape(1), *inputs)


class Ring:
    def __init__(self, size):
        self.size = size
        self.order = [*range(0, size, 2), *range(size - 1, 0, -2)] if size == 8 else list(range(size))
        self.groups = [self.order] if size == 8 else None

    def gather(self, value):
        return lax.all_gather(value, "dp", axis=0, tiled=True, axis_index_groups=self.groups)

    def scatter(self, value):
        total = lax.psum_scatter(value, "dp", scatter_dimension=0, tiled=True, axis_index_groups=self.groups)
        return lax.optimization_barrier(total).astype(F32)

    def inward(self, value, small=False):
        return self.blocks(value, self.order, small)

    def outward(self, value, small=False):
        return self.blocks(value, [self.order.index(d) for d in range(self.size)], small)

    def blocks(self, value, order, small):
        if self.groups is None:
            return value
        rows, width = value.shape
        part = width // self.size
        if small:
            plan = [(0, d * part, k * part, rows, part) for k, d in enumerate(order)]
            return rearrange([value], [value.shape], [[plan]])[0]
        return jnp.concatenate([value[:, d * part : (d + 1) * part] for d in order], axis=1)


def head_columns(index, size, width):
    own = -(-(width // HD) // size)
    even = own - own % 2

    def heads(part, first, count):
        start = min((index * own + first) * HD, width)
        stop = min(start + count * HD, width)
        out = [(0, part * width + start, stop - start), (None, 0, count * HD - stop + start)]
        return [entry for entry in out if entry[2]]

    out = [entry for part in range(3) for entry in heads(part, 0, even)]
    if own % 2:
        out += [entry for part in range(3) for entry in heads(part, even, 1)] + [(None, 0, HD)]
    return out


def hidden_columns(index, size, order, hidden):
    part = hidden // (len(order) * size)
    return [(0, (d * size + index) * part, part) for d in order]


def feature_columns(index, size, order, width, matrix):
    own, part = width // size, width // len(order)
    out, place = [], index * own
    while place < (index + 1) * own:
        stop = min((index + 1) * own, (place // part + 1) * part)
        out.append((matrix, order[place // part] * part + place % part, stop - place))
        place = stop
    return out


def half_masks():
    lane = lax.broadcasted_iota(jnp.int32, (1, LANES), 1)
    return [lane < HD, lane >= HD]


def row_block(ref, block, rows):
    return ref[pl.ds(pl.multiple_of(block * rows, rows), rows), :]


def attention_forward_kernel(size, pairs, odd, info, q_ref, k_ref, v_ref, o_ref, k_all, v_all):
    mine, length = info[0], info[1]
    count = q_ref.shape[0] // size
    pair = pl.program_id(0)
    last = pair == pairs - 1
    for a in range(size):
        rows = pl.ds(a * count, count)
        keys = row_block(k_ref, mine ^ a, count)
        if odd:
            keys = jnp.where(last, jnp.roll(keys, HD, axis=1), keys)
        k_all[rows, :] = keys
        v_all[rows, :] = row_block(v_ref, mine ^ a, count)
    halves = half_masks()
    zero = jnp.zeros((), BF)

    def one(a, half):
        span = (a + 1) * count
        q = jnp.where(half, row_block(q_ref, mine ^ a, count), zero)
        s = lax.dot_general(q, k_all[:span, :], (((1,), (1,)), ((), ())), preferred_element_type=F32) * 0.125
        limit = jnp.minimum(a * count + lax.broadcasted_iota(jnp.int32, (count, 1), 0), length - 1)
        allowed = lax.broadcasted_iota(jnp.int32, (count, span), 1) <= limit
        s = jnp.where(allowed, s, -1e30)
        e = jnp.exp(s - jnp.max(s, axis=1, keepdims=True))
        p = (e * (1.0 / jnp.sum(e, axis=1, keepdims=True))).astype(BF)
        return jnp.dot(p, v_all[:span, :], preferred_element_type=F32)

    for a in range(size):
        rows = pl.ds(pl.multiple_of((mine ^ a) * count, count), count)
        first = one(a, halves[0])
        if not odd:
            o_ref[rows, :] = jnp.where(halves[0], first, one(a, halves[1])).astype(BF)
            continue
        o_ref[rows, :] = jnp.where(halves[0], first, 0.0).astype(BF)

        @pl.when(jnp.logical_not(last))
        def _():
            o_ref[rows, :] = jnp.where(halves[0], o_ref[rows, :], one(a, halves[1]).astype(BF))


def attention_backward_kernel(size, pairs, odd, info, q_ref, k_ref, v_ref, g_ref, d_ref, k_all, v_all, dq, dk, dv):
    mine, length = info[0], info[1]
    count = q_ref.shape[0] // size
    pair = pl.program_id(0)
    last = pair == pairs - 1
    for a in range(size):
        rows = pl.ds(a * count, count)
        keys = row_block(k_ref, mine ^ a, count)
        if odd:
            keys = jnp.where(last, jnp.roll(keys, HD, axis=1), keys)
        k_all[rows, :] = keys
        v_all[rows, :] = row_block(v_ref, mine ^ a, count)
    dk[...] = jnp.zeros_like(dk)
    dv[...] = jnp.zeros_like(dv)
    halves = half_masks()
    zero = jnp.zeros((), BF)

    def one(a, which):
        half = halves[which]
        span = (a + 1) * count
        rows = pl.ds(a * count, count)
        q = jnp.where(half, row_block(q_ref, mine ^ a, count), zero)
        g = jnp.where(half, row_block(g_ref, mine ^ a, count), zero)
        keys, values = k_all[:span, :], v_all[:span, :]
        contract = (((1,), (1,)), ((), ()))
        s = lax.dot_general(keys, q, contract, preferred_element_type=F32) * 0.125
        limit = jnp.minimum(a * count + lax.broadcasted_iota(jnp.int32, (1, count), 1), length - 1)
        allowed = lax.broadcasted_iota(jnp.int32, (span, count), 0) <= limit
        s = jnp.where(allowed, s, -1e30)
        e = jnp.exp(s - jnp.max(s, axis=0, keepdims=True))
        p = e * (1.0 / jnp.sum(e, axis=0, keepdims=True))
        dp = lax.dot_general(values, g, contract, preferred_element_type=F32)
        inner = jnp.sum(p * dp, axis=0, keepdims=True)
        ds = (p * (dp - inner) * 0.125).astype(BF)
        dv[:span, :] += jnp.dot(p.astype(BF), g, preferred_element_type=F32)
        dk[:span, :] += jnp.dot(ds, q, preferred_element_type=F32)
        part = lax.dot_general(ds, keys, (((0,), (0,)), ((), ())), preferred_element_type=F32)
        if which == 0:
            dq[rows, :] = jnp.where(half, part, 0.0)
        else:
            dq[rows, :] = jnp.where(half, part, dq[rows, :])

    for a in range(size):
        one(a, 0)
    if odd:

        @pl.when(jnp.logical_not(last))
        def _():
            for a in range(size):
                one(a, 1)
    else:
        for a in range(size):
            one(a, 1)

    def store(block, value_of):
        cols = pl.ds(pl.multiple_of(block * LANES, LANES), LANES)
        for a in range(size):
            rows = pl.ds(pl.multiple_of((mine ^ a) * count, count), count)
            d_ref[rows, cols] = value_of(pl.ds(a * count, count)).astype(BF)

    full = pairs - 1 if odd else pairs

    def plain():
        store(pair, lambda r: dq[r, :])
        store(full + pair, lambda r: dk[r, :])
        store(2 * full + pair, lambda r: dv[r, :])

    if not odd:
        plain()
        return
    pl.when(jnp.logical_not(last))(plain)

    @pl.when(last)
    def _():
        store(3 * full, lambda r: jnp.where(halves[0], dq[r, :], jnp.roll(dk[r, :], HD, axis=1)))
        store(3 * full + 1, lambda r: jnp.where(halves[0], dv[r, :], 0.0))


def head_specs(span, pairs, odd):
    full = pairs - 1 if odd else pairs

    def spec(part):
        def index(j, info):
            if not odd:
                return (0, part * full + j)
            return (0, jnp.where(j < full, part * full + j, 3 * full + (part == 2)))

        return pl.BlockSpec((span, LANES), index)

    return [spec(0), spec(1), spec(2)]


def attention_forward(info, mixed, own, size):
    span = mixed.shape[0]
    pairs, odd = -(-own // 2), own % 2
    return pl.pallas_call(
        partial(attention_forward_kernel, size, pairs, odd),
        out_shape=jax.ShapeDtypeStruct((span, pairs * LANES), BF),
        grid_spec=pltpu.PrefetchScalarGridSpec(
            num_scalar_prefetch=1,
            grid=(pairs,),
            in_specs=head_specs(span, pairs, odd),
            out_specs=pl.BlockSpec((span, LANES), lambda j, info: (0, j)),
            scratch_shapes=[pltpu.VMEM((span, LANES), BF)] * 2,
        ),
        compiler_params=pltpu.CompilerParams(vmem_limit_bytes=40 << 20),
        cost_estimate=pl.CostEstimate(
            flops=own * span * span * 3400, transcendentals=0, bytes_accessed=mixed.size * 4
        ),
        name="attention_forward",
    )(info, mixed, mixed, mixed)


def attention_backward(info, mixed, grad, own, size):
    span = mixed.shape[0]
    pairs, odd = -(-own // 2), own % 2
    return pl.pallas_call(
        partial(attention_backward_kernel, size, pairs, odd),
        out_shape=jax.ShapeDtypeStruct(mixed.shape, BF),
        grid_spec=pltpu.PrefetchScalarGridSpec(
            num_scalar_prefetch=1,
            grid=(pairs,),
            in_specs=[*head_specs(span, pairs, odd), pl.BlockSpec((span, LANES), lambda j, info: (0, j))],
            out_specs=pl.BlockSpec(mixed.shape, lambda j, info: (0, 0)),
            scratch_shapes=[pltpu.VMEM((span, LANES), BF)] * 2 + [pltpu.VMEM((span, LANES), F32)] * 3,
        ),
        compiler_params=pltpu.CompilerParams(vmem_limit_bytes=48 << 20),
        cost_estimate=pl.CostEstimate(
            flops=own * span * span * 3400, transcendentals=0, bytes_accessed=mixed.size * 6
        ),
        name="attention_backward",
    )(info, mixed, mixed, mixed, grad)


def normal(value):
    centre = value - jnp.mean(value, axis=-1, keepdims=True)
    scale = lax.rsqrt(jnp.mean(centre * centre, axis=-1, keepdims=True) + EPS)
    return centre * scale, scale


def norm_input_grad(unit, scale, gain, grad):
    scaled = grad * gain
    return scale * (
        scaled
        - jnp.mean(scaled, axis=-1, keepdims=True)
        - unit * jnp.mean(scaled * unit, axis=-1, keepdims=True)
    )


ROOT = 0.7978845608028654
CUBIC = 0.044715


def gelu_and_slope(u):
    t = jnp.tanh(ROOT * (u + CUBIC * u * u * u))
    half = 0.5 * (1.0 + t)
    return u * half, half + 0.5 * u * (1.0 - t * t) * ROOT * (1.0 + 3.0 * CUBIC * u * u)


def dot(a, b, dims=((1,), (0,))):
    return lax.dot_general(a, b, (dims, ((), ())), preferred_element_type=F32)


def local(size, dps, tokens, cotangent, lengths, w_qkv, w_out, w_fc, w_proj, attention_vectors, block_vectors):
    _, count, width = tokens.shape
    heads = width // HD
    own = -(-heads // size)
    hidden = w_proj.shape[0] * dps * size // width
    rank = lax.axis_index("seq")
    row = lax.axis_index("dp")
    device = row * size + rank
    devices = dps * size
    length = lengths[0]
    info = jnp.stack([rank.astype(jnp.int32), length])
    unit_rows = width // dps

    links = Links(dps, size)

    ring = Ring(dps)
    quarter = width // size
    columns_qkv = lambda b: head_columns(b, size, width)
    columns_fc = lambda b: hidden_columns(b, size, ring.order, hidden)
    columns_attention = lambda b: columns_qkv(b) + feature_columns(b, size, ring.order, width, 1)

    def own_columns(value, columns):
        count = sum(entry[2] for entry in columns(0))
        plans = [[in_columns(columns(q), 1)] for q in range(size)]
        return rearrange([value.reshape(1, -1)], [(1, count)], plans, rank)[0][0]

    def all_columns(value, total, columns):
        plans = []
        for q in range(size):
            copies = from_columns([columns(q)], 1, 1)[0]
            for b in range(size):
                if b != q:
                    copies += [(None, 0, first, 1, count) for matrix, first, count in columns(b) if matrix is not None]
            plans.append([copies])
        return rearrange([value.reshape(1, -1)], [(1, total)], plans, rank)[0][0]

    split = lambda m: [m[j * count : (j + 1) * count] for j in range(size)]

    attention_part = links.columns_from_rows([w_qkv, w_out], unit_rows, columns_attention)
    attention_full = ring.gather(attention_part)
    qkv_full, out_part = attention_full[:, :-quarter], lax.optimization_barrier(attention_full[:, -quarter:])

    shift = hidden // devices
    tail = -(-shift * devices // LANES) * LANES
    before = links.shift(after(w_fc[-tail:], attention_part), 1)
    part = attention_vectors.shape[0]
    last = device == devices - 1
    small = jnp.zeros((8 * width,), BF)
    small = lax.dynamic_update_slice_in_dim(small, attention_vectors, device * part, 0)
    small = lax.dynamic_update_slice_in_dim(small, block_vectors, 4 * width + device * part, 0)
    small = jnp.concatenate([small, jnp.where(last, w_fc[-hidden:], jnp.zeros((), BF))])
    small = links.all_sum(after(small, attention_part), ("seq", "dp")).astype(F32)
    natural = small[: 8 * width].reshape(8, width)
    gain1, shift1, _, _, bias_o, gain2, shift2, bias_p = ring.inward(natural, small=True)
    bias_fc = own_columns(small[8 * width :], columns_fc)
    bias_qkv = own_columns(jnp.concatenate([natural[2], jnp.zeros_like(natural[2]), natural[3]]), columns_qkv)

    x_own = ring.inward(tokens[0])
    x_all = jnp.concatenate(links.gather_seq(after(x_own, attention_part)), axis=0)
    place = rank * count + jnp.arange(count)
    dy_own = ring.inward(cotangent[0]) * (place < length).astype(BF)[:, None]
    dy_wide = dy_own.astype(F32)
    dy = jnp.concatenate(links.gather_seq(after(dy_own, small, x_all)), axis=0)
    unit1_all, _ = normal(x_all.astype(F32))
    h1 = (unit1_all * gain1 + shift1).astype(BF)
    plain = w_fc.shape[0] - shift
    fc_flat = lax.dynamic_slice_in_dim(jnp.concatenate([before, after(w_fc, attention_part, dy, h1)]), tail - shift * device, plain)
    fc_part = links.columns_from_rows([fc_flat], unit_rows, columns_fc)
    fc_full = ring.gather(fc_part)

    out_parts = links.gather_seq(out_part, free=True)

    mixed = (dot(after(h1, dy), qkv_full) + bias_qkv).astype(BF)
    proj_full = ring.gather(after(ring.inward(w_proj.reshape(-1, width), small=True), fc_part, mixed))
    o_heads = attention_forward(info, mixed, own, size)
    out_parts = [after(piece, mixed) for piece in out_parts]
    o_got = links.relative(links.exchange_seq(split(o_heads)))
    o_own = jnp.concatenate([piece[:, : own * HD] for piece in o_got], axis=1)
    o_own = ring.inward(o_own[:, :width])
    projected = links.relative([dot(o_own, piece) for piece in out_parts])
    x2 = x_own.astype(F32) + jnp.concatenate(projected, axis=1) + bias_o
    unit2, scale2 = normal(x2)
    h2 = jnp.concatenate(links.gather_seq((unit2 * gain2 + shift2).astype(BF)), axis=0)

    u = dot(h2, fc_full) + bias_fc
    a, slope = gelu_and_slope(u)
    a, slope = a.astype(BF), slope.astype(BF)
    grad_proj = dot(a, dy, ((0,), (0,))).astype(BF)
    grad_proj_own = ring.scatter(grad_proj)
    du = (dot(after(dy, grad_proj), proj_full, ((1,), (1,))) * slope.astype(F32)).astype(BF)
    dh2_part = dot(du, fc_full, ((1,), (1,)))
    dh2 = links.scatter_seq(split(dh2_part))
    grad_fc = dot(h2, after(du, dh2_part), ((0,), (0,))).astype(BF)
    output_part = dot(after(a, grad_fc), proj_full)
    dh2 = after(dh2, output_part)
    grad_fc = ring.scatter(after(grad_fc, grad_proj_own))
    dx2 = dy_wide + norm_input_grad(unit2, scale2, gain2, dh2)
    dz = dx2.astype(BF)

    dz_parts = links.relative([dz[:, b * quarter : (b + 1) * quarter] for b in range(size)])
    do_own = sum(dot(dz_part, piece, ((1,), (1,))) for dz_part, piece in zip(dz_parts, out_parts))
    do_own = jnp.pad(ring.outward(do_own.astype(BF)), ((0, 0), (0, own * size * HD - width)))
    do_blocks = [jnp.pad(do_own[:, b * own * HD : (b + 1) * own * HD], ((0, 0), (0, own % 2 * HD))) for b in range(size)]
    do_heads = jnp.concatenate(links.exchange_seq(links.relative(do_blocks)), axis=0)
    grad_out = [dot(after(o_own, do_own), dz_part, ((0,), (0,))).astype(BF) for dz_part in dz_parts]
    do_heads = after(do_heads, *grad_out, grad_proj_own)
    dmixed = attention_backward(info, mixed, do_heads, own, size)
    grad_out = links.scatter_seq(grad_out, dmixed, free=True).astype(BF)
    dh1_part = dot(dmixed, qkv_full, ((1,), (1,)))
    grad_qkv = dot(h1, after(dmixed, dh1_part), ((0,), (0,))).astype(BF)
    grad_attention = jnp.concatenate([grad_qkv, grad_out], axis=1)
    dh1_part, dmixed, grad_fc = (after(value, grad_attention) for value in (dh1_part, dmixed, grad_fc))
    output = links.scatter_seq(split(output_part), free=True, hold=grad_attention)
    output = ring.outward((x2 + output + bias_p).astype(BF))
    grad_attention = ring.scatter(grad_attention)
    fc_rows = links.rows_from_columns(grad_fc, [hidden], columns_fc)[0]
    behind = links.shift(fc_rows[:tail].astype(BF), -1)
    total = lambda m: jnp.sum(m.astype(F32), axis=0)
    wide = all_columns(total(dmixed), 3 * width, columns_qkv)
    inner = [total(dh1_part * unit1_all), total(dh1_part), total(dz), total(dh2 * unit2), total(dh2), total(dy_wide)]
    grad_g1, grad_c1, grad_bo, grad_g2, grad_c2, grad_bp = ring.outward(jnp.stack(inner), small=True)
    sums = jnp.concatenate([
        grad_g1, grad_c1, wide[:width], wide[2 * width :], grad_bo, grad_g2, grad_c2, grad_bp,
        all_columns(total(after(du, grad_fc)), hidden, columns_fc),
    ])
    sums = links.all_sum(sums, ("seq",), free=True)
    dh1 = links.scatter_seq(split(dh1_part), free=True, hold=sums)
    qkv_flat, out_flat = links.rows_from_columns(grad_attention, [3 * width, width], columns_attention)
    dh1 = after(dh1, *links.sent)
    unit1, scale1 = normal(x_own.astype(F32))
    input_grad = ring.outward(dx2 + norm_input_grad(unit1, scale1, gain1, dh1))

    sums = links.all_sum(sums, ("dp",), free=True)
    vec1 = lax.dynamic_slice_in_dim(sums[: 4 * width], device * part, part)
    vec2 = lax.dynamic_slice_in_dim(sums[4 * width : 8 * width], device * part, part)
    sum_bf = sums[8 * width :]

    behind = jnp.where(last, jnp.pad(sum_bf, (0, tail - hidden)), behind.astype(F32))
    fc_flat_grad = lax.dynamic_slice_in_dim(
        jnp.concatenate([fc_rows, behind]), shift * device, w_fc.shape[0]
    )
    grad_attention = after(grad_attention, input_grad, fc_flat_grad, vec1, vec2, output)
    return (output[None], input_grad[None], qkv_flat, out_flat, fc_flat_grad, ring.outward(grad_proj_own, small=True).reshape(-1), vec1, vec2)


def solution(mesh):
    tokens = P("dp", "seq", None)
    flat = P(("dp", "seq"))
    return jax.shard_map(
        partial(local, mesh.shape["seq"], mesh.shape["dp"]),
        mesh=mesh,
        in_specs=(tokens, tokens, P("dp"), *[flat] * 6),
        out_specs=(tokens, tokens, *[flat] * 6),
        check_vma=False,
    )
```

```python
from functools import partial

import jax
import jax.numpy as jnp
from jax import lax
from jax.experimental import pallas as pl
from jax.experimental.pallas import tpu as pltpu
from jax.sharding import PartitionSpec as P

HD = 64
EPS = 1e-05
LANES = 128
BF = jnp.bfloat16
F32 = jnp.float32


def bits_of(size):
    return [1 << k for k in reversed(range(size.bit_length() - 1))]


def after(value, *others):
    others = [o for o in others if o is not None]
    return lax.optimization_barrier((value, *others))[0] if others else value


def pick(pieces, index):
    out = pieces[0]
    for k in range(1, len(pieces)):
        out = jnp.where(index == k, pieces[k], out)
    return out


class Links:
    def __init__(self, dps, seqs):
        self.sizes = {"dp": dps, "seq": seqs}
        self.last = {}
        self.sent = []

    def ordered(self, value, link, permute):
        self.last[link] = permute(after(value, self.last.get(link)))
        return self.last[link]

    def swap(self, value, axis, bits, free=False):
        pairs = [(i, i ^ bits) for i in range(self.sizes[axis])]
        if free:
            return lax.ppermute(value, axis, pairs)
        top = 1 << (bits.bit_length() - 1)
        return self.ordered(value, (axis, top), lambda v: lax.ppermute(v, axis, pairs))

    def shift(self, value, step):
        count = self.sizes["dp"] * self.sizes["seq"]
        pairs = [(i, i + step) for i in range(count) if 0 <= i + step < count]
        return self.ordered(value, ("seq", 1), lambda v: lax.ppermute(v, ("dp", "seq"), pairs))

    def all_sum(self, value, axes, free=False):
        for axis in axes:
            for bit in bits_of(self.sizes[axis]):
                value = value + self.swap(value, axis, bit, free)
        return value

    def gather_seq(self, value, free=False):
        pieces = {0: value}
        for bit in bits_of(self.sizes["seq"]):
            for j in list(pieces):
                pieces[j ^ bit] = self.swap(pieces[j], "seq", bit, free)
        return [pieces[j] for j in range(len(pieces))]

    def scatter_seq(self, blocks, last=None, free=False, hold=None):
        blocks = dict(enumerate(blocks))
        for bit in reversed(bits_of(self.sizes["seq"])):
            for j in sorted(blocks, reverse=True):
                if j & bit:
                    final = j == bit and j > 1
                    sent = after(blocks.pop(j).astype(BF), hold if final else None)
                    got = after(self.swap(sent, "seq", bit, free), last if final else None)
                    blocks[j ^ bit] = blocks[j ^ bit].astype(F32) + got.astype(F32)
        return blocks[0]

    def exchange_seq(self, pieces):
        return [pieces[0]] + [self.swap(pieces[j], "seq", j, True) for j in range(1, len(pieces))]

    def relative(self, pieces, axis="seq"):
        mine, size = lax.axis_index(axis), len(pieces)
        return [pick([pieces[j ^ m] for m in range(size)], mine) for j in range(size)]

    def columns_from_rows(self, flats, rows, columns):
        size, rank = self.sizes["seq"], lax.axis_index("seq")
        shape = lambda flat: (-1, flat.shape[0] * size // rows)
        own = sum(count for _, _, count in columns(0))
        if rows % size == 0:
            part = rows // size
            plans = [[in_columns(columns(q ^ j), part) for j in range(size)] for q in range(size)]
            pieces = rearrange([flat.reshape(shape(flat)) for flat in flats], [(part, own)] * size, plans, rank)
            return jnp.concatenate(self.relative(self.exchange_seq(pieces)), axis=0)
        full = [lax.all_gather(flat, "seq", axis=0, tiled=True).reshape(shape(flat)) for flat in flats]
        return rearrange(full, [(rows, own)], [[in_columns(columns(q), rows)] for q in range(size)], rank)[0]

    def rows_from_columns(self, value, widths, columns):
        size, rank = self.sizes["seq"], lax.axis_index("seq")
        rows = value.shape[0]
        value = value.astype(BF)
        if rows % size == 0:
            part = rows // size
            pieces = self.relative([value[b * part : (b + 1) * part] for b in range(size)])
            self.sent = pieces
            plans = [from_columns([columns(q ^ j) for j in range(size)], part, len(widths)) for q in range(size)]
            out = rearrange(self.exchange_seq(pieces), [(part, w) for w in widths], plans, rank, F32)
            return [matrix.reshape(-1) for matrix in out]
        full = lax.all_gather(value, "seq", axis=0, tiled=False)
        plans = [from_columns([columns(b) for b in range(size)], rows, len(widths))]
        out = []
        for matrix in rearrange([full[b] for b in range(size)], [(rows, w) for w in widths], plans, dtype=F32):
            count = matrix.size // size
            out.append(lax.dynamic_slice_in_dim(matrix.reshape(-1), rank * count, count))
        return out


def in_columns(columns, rows):
    copies, place = [], 0
    for matrix, first, count in columns:
        copies.append((matrix, first, place, rows, count))
        place += count
    return copies


def from_columns(columns_of, rows, matrices):
    out = [[] for _ in range(matrices)]
    for which, columns in enumerate(columns_of):
        place = 0
        for matrix, first, count in columns:
            if matrix is not None:
                out[matrix].append((which, place, first, rows, count))
            place += count
    return out


def rearrange_kernel(plans, count, info, *refs):
    inputs, outputs = refs[:count], refs[count:]

    def run(plan):
        for out, copies in zip(outputs, plan):
            for which, first, place, rows, columns in copies:
                if which is None:
                    value = jnp.zeros((rows, columns), out.dtype)
                else:
                    value = inputs[which][:rows, first : first + columns].astype(out.dtype)
                out[:rows, place : place + columns] = value

    if len(plans) == 1:
        run(plans[0])
        return
    for rank, plan in enumerate(plans):
        pl.when(info[0] == rank)(partial(run, plan))


def rearrange(inputs, shapes, plans, rank=0, dtype=None):
    dtype = dtype or inputs[0].dtype
    spec = lambda shape: pl.BlockSpec(shape, lambda i, info: (0, 0))
    return pl.pallas_call(
        partial(rearrange_kernel, plans, len(inputs)),
        out_shape=[jax.ShapeDtypeStruct(shape, dtype) for shape in shapes],
        grid_spec=pltpu.PrefetchScalarGridSpec(
            num_scalar_prefetch=1,
            grid=(1,),
            in_specs=[spec(value.shape) for value in inputs],
            out_specs=[spec(shape) for shape in shapes],
        ),
        compiler_params=pltpu.CompilerParams(vmem_limit_bytes=40 << 20),
        cost_estimate=pl.CostEstimate(
            flops=0, transcendentals=0, bytes_accessed=2 * sum(value.size * value.dtype.itemsize for value in inputs)
        ),
        name="rearrange",
    )(jnp.asarray(rank, jnp.int32).reshape(1), *inputs)


class Ring:
    def __init__(self, size):
        self.size = size
        self.order = [*range(0, size, 2), *range(size - 1, 0, -2)] if size == 8 else list(range(size))
        self.groups = [self.order] if size == 8 else None

    def gather(self, value):
        return lax.all_gather(value, "dp", axis=0, tiled=True, axis_index_groups=self.groups)

    def scatter(self, value):
        total = lax.psum_scatter(value, "dp", scatter_dimension=0, tiled=True, axis_index_groups=self.groups)
        return lax.optimization_barrier(total)

    def inward(self, value, small=False):
        return self.blocks(value, self.order, small)

    def outward(self, value, small=False):
        return self.blocks(value, [self.order.index(d) for d in range(self.size)], small)

    def blocks(self, value, order, small):
        if self.groups is None:
            return value
        rows, width = value.shape
        part = width // self.size
        if small:
            plan = [(0, d * part, k * part, rows, part) for k, d in enumerate(order)]
            return rearrange([value], [value.shape], [[plan]])[0]
        return jnp.concatenate([value[:, d * part : (d + 1) * part] for d in order], axis=1)


def head_columns(index, size, width):
    own = -(-(width // HD) // size)
    even = own - own % 2

    def heads(part, first, count):
        start = min((index * own + first) * HD, width)
        stop = min(start + count * HD, width)
        out = [(0, part * width + start, stop - start), (None, 0, count * HD - stop + start)]
        return [entry for entry in out if entry[2]]

    out = [entry for part in range(3) for entry in heads(part, 0, even)]
    if own % 2:
        out += [entry for part in range(3) for entry in heads(part, even, 1)] + [(None, 0, HD)]
    return out


def hidden_columns(index, size, order, hidden):
    part = hidden // (len(order) * size)
    return [(0, (d * size + index) * part, part) for d in order]


def feature_columns(index, size, order, width, matrix):
    own, part = width // size, width // len(order)
    out, place = [], index * own
    while place < (index + 1) * own:
        stop = min((index + 1) * own, (place // part + 1) * part)
        out.append((matrix, order[place // part] * part + place % part, stop - place))
        place = stop
    return out


def half_masks():
    lane = lax.broadcasted_iota(jnp.int32, (1, LANES), 1)
    return [lane < HD, lane >= HD]


def row_block(ref, block, rows):
    return ref[pl.ds(pl.multiple_of(block * rows, rows), rows), :]


def attention_forward_kernel(size, pairs, odd, info, q_ref, k_ref, v_ref, o_ref, k_all, v_all):
    mine, length = info[0], info[1]
    count = q_ref.shape[0] // size
    pair = pl.program_id(0)
    last = pair == pairs - 1
    for a in range(size):
        rows = pl.ds(a * count, count)
        keys = row_block(k_ref, mine ^ a, count)
        if odd:
            keys = jnp.where(last, jnp.roll(keys, HD, axis=1), keys)
        k_all[rows, :] = keys
        v_all[rows, :] = row_block(v_ref, mine ^ a, count)
    halves = half_masks()
    zero = jnp.zeros((), BF)

    def one(a, half):
        span = (a + 1) * count
        q = jnp.where(half, row_block(q_ref, mine ^ a, count), zero)
        s = lax.dot_general(q, k_all[:span, :], (((1,), (1,)), ((), ())), preferred_element_type=F32) * 0.125
        limit = jnp.minimum(a * count + lax.broadcasted_iota(jnp.int32, (count, 1), 0), length - 1)
        allowed = lax.broadcasted_iota(jnp.int32, (count, span), 1) <= limit
        s = jnp.where(allowed, s, -1e30)
        e = jnp.exp(s - jnp.max(s, axis=1, keepdims=True))
        p = (e * (1.0 / jnp.sum(e, axis=1, keepdims=True))).astype(BF)
        return jnp.dot(p, v_all[:span, :], preferred_element_type=F32)

    for a in range(size):
        rows = pl.ds(pl.multiple_of((mine ^ a) * count, count), count)
        first = one(a, halves[0])
        if not odd:
            o_ref[rows, :] = jnp.where(halves[0], first, one(a, halves[1])).astype(BF)
            continue
        o_ref[rows, :] = jnp.where(halves[0], first, 0.0).astype(BF)

        @pl.when(jnp.logical_not(last))
        def _():
            o_ref[rows, :] = jnp.where(halves[0], o_ref[rows, :], one(a, halves[1]).astype(BF))


def attention_backward_kernel(size, pairs, odd, info, q_ref, k_ref, v_ref, g_ref, d_ref, k_all, v_all, dq, dk, dv):
    mine, length = info[0], info[1]
    count = q_ref.shape[0] // size
    pair = pl.program_id(0)
    last = pair == pairs - 1
    for a in range(size):
        rows = pl.ds(a * count, count)
        keys = row_block(k_ref, mine ^ a, count)
        if odd:
            keys = jnp.where(last, jnp.roll(keys, HD, axis=1), keys)
        k_all[rows, :] = keys
        v_all[rows, :] = row_block(v_ref, mine ^ a, count)
    dk[...] = jnp.zeros_like(dk)
    dv[...] = jnp.zeros_like(dv)
    halves = half_masks()
    zero = jnp.zeros((), BF)

    def one(a, which):
        half = halves[which]
        span = (a + 1) * count
        rows = pl.ds(a * count, count)
        q = jnp.where(half, row_block(q_ref, mine ^ a, count), zero)
        g = jnp.where(half, row_block(g_ref, mine ^ a, count), zero)
        keys, values = k_all[:span, :], v_all[:span, :]
        contract = (((1,), (1,)), ((), ()))
        s = lax.dot_general(keys, q, contract, preferred_element_type=F32) * 0.125
        limit = jnp.minimum(a * count + lax.broadcasted_iota(jnp.int32, (1, count), 1), length - 1)
        allowed = lax.broadcasted_iota(jnp.int32, (span, count), 0) <= limit
        s = jnp.where(allowed, s, -1e30)
        e = jnp.exp(s - jnp.max(s, axis=0, keepdims=True))
        p = e * (1.0 / jnp.sum(e, axis=0, keepdims=True))
        dp = lax.dot_general(values, g, contract, preferred_element_type=F32)
        inner = jnp.sum(p * dp, axis=0, keepdims=True)
        ds = (p * (dp - inner) * 0.125).astype(BF)
        dv[:span, :] += jnp.dot(p.astype(BF), g, preferred_element_type=F32)
        dk[:span, :] += jnp.dot(ds, q, preferred_element_type=F32)
        part = lax.dot_general(ds, keys, (((0,), (0,)), ((), ())), preferred_element_type=F32)
        if which == 0:
            dq[rows, :] = jnp.where(half, part, 0.0)
        else:
            dq[rows, :] = jnp.where(half, part, dq[rows, :])

    for a in range(size):
        one(a, 0)
    if odd:

        @pl.when(jnp.logical_not(last))
        def _():
            for a in range(size):
                one(a, 1)
    else:
        for a in range(size):
            one(a, 1)

    def store(block, value_of):
        cols = pl.ds(pl.multiple_of(block * LANES, LANES), LANES)
        for a in range(size):
            rows = pl.ds(pl.multiple_of((mine ^ a) * count, count), count)
            d_ref[rows, cols] = value_of(pl.ds(a * count, count)).astype(BF)

    full = pairs - 1 if odd else pairs

    def plain():
        store(pair, lambda r: dq[r, :])
        store(full + pair, lambda r: dk[r, :])
        store(2 * full + pair, lambda r: dv[r, :])

    if not odd:
        plain()
        return
    pl.when(jnp.logical_not(last))(plain)

    @pl.when(last)
    def _():
        store(3 * full, lambda r: jnp.where(halves[0], dq[r, :], jnp.roll(dk[r, :], HD, axis=1)))
        store(3 * full + 1, lambda r: jnp.where(halves[0], dv[r, :], 0.0))


def head_specs(span, pairs, odd):
    full = pairs - 1 if odd else pairs

    def spec(part):
        def index(j, info):
            if not odd:
                return (0, part * full + j)
            return (0, jnp.where(j < full, part * full + j, 3 * full + (part == 2)))

        return pl.BlockSpec((span, LANES), index)

    return [spec(0), spec(1), spec(2)]


def attention_forward(info, mixed, own, size):
    span = mixed.shape[0]
    pairs, odd = -(-own // 2), own % 2
    return pl.pallas_call(
        partial(attention_forward_kernel, size, pairs, odd),
        out_shape=jax.ShapeDtypeStruct((span, pairs * LANES), BF),
        grid_spec=pltpu.PrefetchScalarGridSpec(
            num_scalar_prefetch=1,
            grid=(pairs,),
            in_specs=head_specs(span, pairs, odd),
            out_specs=pl.BlockSpec((span, LANES), lambda j, info: (0, j)),
            scratch_shapes=[pltpu.VMEM((span, LANES), BF)] * 2,
        ),
        compiler_params=pltpu.CompilerParams(vmem_limit_bytes=40 << 20),
        cost_estimate=pl.CostEstimate(
            flops=own * span * span * 3400, transcendentals=0, bytes_accessed=mixed.size * 4
        ),
        name="attention_forward",
    )(info, mixed, mixed, mixed)


def attention_backward(info, mixed, grad, own, size):
    span = mixed.shape[0]
    pairs, odd = -(-own // 2), own % 2
    return pl.pallas_call(
        partial(attention_backward_kernel, size, pairs, odd),
        out_shape=jax.ShapeDtypeStruct(mixed.shape, BF),
        grid_spec=pltpu.PrefetchScalarGridSpec(
            num_scalar_prefetch=1,
            grid=(pairs,),
            in_specs=[*head_specs(span, pairs, odd), pl.BlockSpec((span, LANES), lambda j, info: (0, j))],
            out_specs=pl.BlockSpec(mixed.shape, lambda j, info: (0, 0)),
            scratch_shapes=[pltpu.VMEM((span, LANES), BF)] * 2 + [pltpu.VMEM((span, LANES), F32)] * 3,
        ),
        compiler_params=pltpu.CompilerParams(vmem_limit_bytes=48 << 20),
        cost_estimate=pl.CostEstimate(
            flops=own * span * span * 3400, transcendentals=0, bytes_accessed=mixed.size * 6
        ),
        name="attention_backward",
    )(info, mixed, mixed, mixed, grad)


def normal(value):
    centre = value - jnp.mean(value, axis=-1, keepdims=True)
    scale = lax.rsqrt(jnp.mean(centre * centre, axis=-1, keepdims=True) + EPS)
    return centre * scale, scale


def norm_input_grad(unit, scale, gain, grad):
    scaled = grad * gain
    return scale * (
        scaled
        - jnp.mean(scaled, axis=-1, keepdims=True)
        - unit * jnp.mean(scaled * unit, axis=-1, keepdims=True)
    )


ROOT = 0.7978845608028654
CUBIC = 0.044715


def gelu_and_slope(u):
    t = jnp.tanh(ROOT * (u + CUBIC * u * u * u))
    half = 0.5 * (1.0 + t)
    return u * half, half + 0.5 * u * (1.0 - t * t) * ROOT * (1.0 + 3.0 * CUBIC * u * u)


def dot(a, b, dims=((1,), (0,))):
    return lax.dot_general(a, b, (dims, ((), ())), preferred_element_type=F32)


def local(size, dps, tokens, cotangent, lengths, w_qkv, w_out, w_fc, w_proj, attention_vectors, block_vectors):
    _, count, width = tokens.shape
    heads = width // HD
    own = -(-heads // size)
    hidden = w_proj.shape[0] * dps * size // width
    rank = lax.axis_index("seq")
    row = lax.axis_index("dp")
    device = row * size + rank
    devices = dps * size
    length = lengths[0]
    info = jnp.stack([rank.astype(jnp.int32), length])
    unit_rows = width // dps

    links = Links(dps, size)

    ring = Ring(dps)
    quarter = width // size
    columns_qkv = lambda b: head_columns(b, size, width)
    columns_fc = lambda b: hidden_columns(b, size, ring.order, hidden)
    columns_attention = lambda b: columns_qkv(b) + feature_columns(b, size, ring.order, width, 1)

    def own_columns(value, columns):
        count = sum(entry[2] for entry in columns(0))
        plans = [[in_columns(columns(q), 1)] for q in range(size)]
        return rearrange([value.reshape(1, -1)], [(1, count)], plans, rank)[0][0]

    def all_columns(value, total, columns):
        plans = []
        for q in range(size):
            copies = from_columns([columns(q)], 1, 1)[0]
            for b in range(size):
                if b != q:
                    copies += [(None, 0, first, 1, count) for matrix, first, count in columns(b) if matrix is not None]
            plans.append([copies])
        return rearrange([value.reshape(1, -1)], [(1, total)], plans, rank)[0][0]

    split = lambda m: [m[j * count : (j + 1) * count] for j in range(size)]

    attention_part = links.columns_from_rows([w_qkv, w_out], unit_rows, columns_attention)
    attention_full = ring.gather(attention_part)
    qkv_full, out_part = attention_full[:, :-quarter], lax.optimization_barrier(attention_full[:, -quarter:])

    shift = hidden // devices
    tail = -(-shift * devices // LANES) * LANES
    before = links.shift(after(w_fc[-tail:], attention_part), 1)
    part = attention_vectors.shape[0]
    last = device == devices - 1
    small = jnp.zeros((8 * width,), BF)
    small = lax.dynamic_update_slice_in_dim(small, attention_vectors, device * part, 0)
    small = lax.dynamic_update_slice_in_dim(small, block_vectors, 4 * width + device * part, 0)
    small = jnp.concatenate([small, jnp.where(last, w_fc[-hidden:], jnp.zeros((), BF))])
    small = links.all_sum(after(small, attention_part), ("seq", "dp")).astype(F32)
    natural = small[: 8 * width].reshape(8, width)
    gain1, shift1, _, _, bias_o, gain2, shift2, bias_p = ring.inward(natural, small=True)
    bias_fc = own_columns(small[8 * width :], columns_fc)
    bias_qkv = own_columns(jnp.concatenate([natural[2], jnp.zeros_like(natural[2]), natural[3]]), columns_qkv)

    x_own = ring.inward(tokens[0])
    x_all = jnp.concatenate(links.gather_seq(after(x_own, attention_part)), axis=0)
    place = rank * count + jnp.arange(count)
    dy_own = ring.inward(cotangent[0]) * (place < length).astype(BF)[:, None]
    dy_wide = dy_own.astype(F32)
    dy = jnp.concatenate(links.gather_seq(after(dy_own, small, x_all)), axis=0)
    unit1_all, _ = normal(x_all.astype(F32))
    h1 = (unit1_all * gain1 + shift1).astype(BF)
    plain = w_fc.shape[0] - shift
    fc_flat = lax.dynamic_slice_in_dim(jnp.concatenate([before, after(w_fc, attention_part, dy, h1)]), tail - shift * device, plain)
    fc_part = links.columns_from_rows([fc_flat], unit_rows, columns_fc)
    fc_full = ring.gather(fc_part)

    out_parts = links.gather_seq(out_part, free=True)

    mixed = (dot(after(h1, dy), qkv_full) + bias_qkv).astype(BF)
    proj_full = ring.gather(after(ring.inward(w_proj.reshape(-1, width), small=True), fc_part, mixed))
    o_heads = attention_forward(info, mixed, own, size)
    out_parts = [after(piece, mixed) for piece in out_parts]
    o_got = links.relative(links.exchange_seq(split(o_heads)))
    o_own = jnp.concatenate([piece[:, : own * HD] for piece in o_got], axis=1)
    o_own = ring.inward(o_own[:, :width])
    projected = links.relative([dot(o_own, piece) for piece in out_parts])
    x2 = x_own.astype(F32) + jnp.concatenate(projected, axis=1) + bias_o
    unit2, scale2 = normal(x2)
    h2 = jnp.concatenate(links.gather_seq((unit2 * gain2 + shift2).astype(BF)), axis=0)

    u = dot(h2, fc_full) + bias_fc
    a, slope = gelu_and_slope(u)
    a, slope = a.astype(BF), slope.astype(BF)
    grad_proj = dot(a, dy, ((0,), (0,))).astype(BF)
    grad_proj_own = ring.scatter(grad_proj)
    du = (dot(after(dy, grad_proj), proj_full, ((1,), (1,))) * slope.astype(F32)).astype(BF)
    dh2_part = dot(du, fc_full, ((1,), (1,)))
    dh2 = links.scatter_seq(split(dh2_part))
    grad_fc = dot(h2, after(du, dh2_part), ((0,), (0,))).astype(BF)
    output_part = dot(after(a, grad_fc), proj_full)
    dh2 = after(dh2, output_part)
    grad_fc = ring.scatter(after(grad_fc, grad_proj_own))
    dx2 = dy_wide + norm_input_grad(unit2, scale2, gain2, dh2)
    dz = dx2.astype(BF)

    dz_parts = links.relative([dz[:, b * quarter : (b + 1) * quarter] for b in range(size)])
    do_own = sum(dot(dz_part, piece, ((1,), (1,))) for dz_part, piece in zip(dz_parts, out_parts))
    do_own = jnp.pad(ring.outward(do_own.astype(BF)), ((0, 0), (0, own * size * HD - width)))
    do_blocks = [jnp.pad(do_own[:, b * own * HD : (b + 1) * own * HD], ((0, 0), (0, own % 2 * HD))) for b in range(size)]
    do_blocks = links.relative(do_blocks)
    do_heads = jnp.concatenate(links.exchange_seq(do_blocks), axis=0)
    grad_out = [dot(after(o_own, *do_blocks), dz_part, ((0,), (0,))).astype(BF) for dz_part in dz_parts]
    do_heads = after(do_heads, *grad_out, grad_proj_own)
    dmixed = attention_backward(info, mixed, do_heads, own, size)
    grad_out = links.scatter_seq(grad_out, dmixed, free=True).astype(BF)
    dh1_part = dot(dmixed, qkv_full, ((1,), (1,)))
    grad_qkv = dot(h1, after(dmixed, dh1_part), ((0,), (0,))).astype(BF)
    grad_attention = jnp.concatenate([grad_qkv, grad_out], axis=1)
    dh1_part, dmixed, grad_fc = (after(value, grad_attention) for value in (dh1_part, dmixed, grad_fc))
    output = links.scatter_seq(split(output_part), free=True, hold=grad_attention)
    output = ring.outward((x2 + output + bias_p).astype(BF))
    grad_attention = ring.scatter(grad_attention)
    fc_rows = links.rows_from_columns(grad_fc, [hidden], columns_fc)[0]
    behind = links.shift(fc_rows[:tail].astype(BF), -1)
    total = lambda m: jnp.sum(m.astype(F32), axis=0)
    wide = all_columns(total(dmixed), 3 * width, columns_qkv)
    inner = [total(dh1_part * unit1_all), total(dh1_part), total(dz), total(dh2 * unit2), total(dh2), total(dy_wide)]
    grad_g1, grad_c1, grad_bo, grad_g2, grad_c2, grad_bp = ring.outward(jnp.stack(inner), small=True)
    sums = jnp.concatenate([
        grad_g1, grad_c1, wide[:width], wide[2 * width :], grad_bo, grad_g2, grad_c2, grad_bp,
        all_columns(total(after(du, grad_fc)), hidden, columns_fc),
    ])
    sums = links.all_sum(sums, ("seq",), free=True)
    dh1 = links.scatter_seq(split(dh1_part), free=True, hold=sums)
    qkv_flat, out_flat = links.rows_from_columns(grad_attention, [3 * width, width], columns_attention)
    dh1 = after(dh1, *links.sent)
    unit1, scale1 = normal(x_own.astype(F32))
    input_grad = ring.outward(dx2 + norm_input_grad(unit1, scale1, gain1, dh1))

    sums = links.all_sum(sums, ("dp",), free=True)
    vec1 = lax.dynamic_slice_in_dim(sums[: 4 * width], device * part, part)
    vec2 = lax.dynamic_slice_in_dim(sums[4 * width : 8 * width], device * part, part)
    sum_bf = sums[8 * width :]

    behind = jnp.where(last, jnp.pad(sum_bf, (0, tail - hidden)), behind.astype(F32))
    fc_flat_grad = lax.dynamic_slice_in_dim(
        jnp.concatenate([fc_rows, behind]), shift * device, w_fc.shape[0]
    )
    grad_attention = after(grad_attention, input_grad, fc_flat_grad, vec1, vec2, output)
    return (output[None], input_grad[None], qkv_flat, out_flat, fc_flat_grad, ring.outward(grad_proj_own, small=True).astype(F32).reshape(-1), vec1, vec2)


def solution(mesh):
    tokens = P("dp", "seq", None)
    flat = P(("dp", "seq"))
    return jax.shard_map(
        partial(local, mesh.shape["seq"], mesh.shape["dp"]),
        mesh=mesh,
        in_specs=(tokens, tokens, P("dp"), *[flat] * 6),
        out_specs=(tokens, tokens, *[flat] * 6),
        check_vma=False,
    )
```

```python
from functools import partial

import jax
import jax.numpy as jnp
from jax import lax
from jax.experimental import pallas as pl
from jax.experimental.pallas import tpu as pltpu
from jax.sharding import PartitionSpec as P

HD = 64
EPS = 1e-05
LANES = 128
BF = jnp.bfloat16
F32 = jnp.float32


def bits_of(size):
    return [1 << k for k in reversed(range(size.bit_length() - 1))]


def after(value, *others):
    others = [o for o in others if o is not None]
    return lax.optimization_barrier((value, *others))[0] if others else value


def pick(pieces, index):
    out = pieces[0]
    for k in range(1, len(pieces)):
        out = jnp.where(index == k, pieces[k], out)
    return out


class Links:
    def __init__(self, dps, seqs):
        self.sizes = {"dp": dps, "seq": seqs}
        self.last = {}
        self.sent = []

    def ordered(self, value, link, permute):
        self.last[link] = permute(after(value, self.last.get(link)))
        return self.last[link]

    def swap(self, value, axis, bits, free=False):
        pairs = [(i, i ^ bits) for i in range(self.sizes[axis])]
        if free:
            return lax.ppermute(value, axis, pairs)
        top = 1 << (bits.bit_length() - 1)
        return self.ordered(value, (axis, top), lambda v: lax.ppermute(v, axis, pairs))

    def shift(self, value, step):
        count = self.sizes["dp"] * self.sizes["seq"]
        pairs = [(i, i + step) for i in range(count) if 0 <= i + step < count]
        return self.ordered(value, ("seq", 1), lambda v: lax.ppermute(v, ("dp", "seq"), pairs))

    def all_sum(self, value, axes, free=False):
        for axis in axes:
            for bit in bits_of(self.sizes[axis]):
                value = value + self.swap(value, axis, bit, free)
        return value

    def gather_seq(self, value, free=False):
        pieces = {0: value}
        for bit in bits_of(self.sizes["seq"]):
            for j in list(pieces):
                pieces[j ^ bit] = self.swap(pieces[j], "seq", bit, free)
        return [pieces[j] for j in range(len(pieces))]

    def scatter_seq(self, blocks, last=None, free=False, hold=None):
        blocks = dict(enumerate(blocks))
        for bit in reversed(bits_of(self.sizes["seq"])):
            for j in sorted(blocks, reverse=True):
                if j & bit:
                    final = j == bit and j > 1
                    sent = after(blocks.pop(j).astype(BF), hold if final else None)
                    got = after(self.swap(sent, "seq", bit, free), last if final else None)
                    blocks[j ^ bit] = blocks[j ^ bit].astype(F32) + got.astype(F32)
        return blocks[0]

    def exchange_seq(self, pieces):
        return [pieces[0]] + [self.swap(pieces[j], "seq", j, True) for j in range(1, len(pieces))]

    def relative(self, pieces, axis="seq"):
        mine, size = lax.axis_index(axis), len(pieces)
        return [pick([pieces[j ^ m] for m in range(size)], mine) for j in range(size)]

    def columns_from_rows(self, flats, rows, columns):
        size, rank = self.sizes["seq"], lax.axis_index("seq")
        shape = lambda flat: (-1, flat.shape[0] * size // rows)
        own = sum(count for _, _, count in columns(0))
        if rows % size == 0:
            part = rows // size
            plans = [[in_columns(columns(q ^ j), part) for j in range(size)] for q in range(size)]
            pieces = rearrange([flat.reshape(shape(flat)) for flat in flats], [(part, own)] * size, plans, rank)
            return jnp.concatenate(self.relative(self.exchange_seq(pieces)), axis=0)
        full = [lax.all_gather(flat, "seq", axis=0, tiled=True).reshape(shape(flat)) for flat in flats]
        return rearrange(full, [(rows, own)], [[in_columns(columns(q), rows)] for q in range(size)], rank)[0]

    def rows_from_columns(self, value, widths, columns):
        size, rank = self.sizes["seq"], lax.axis_index("seq")
        rows = value.shape[0]
        value = value.astype(BF)
        if rows % size == 0:
            part = rows // size
            pieces = self.relative([value[b * part : (b + 1) * part] for b in range(size)])
            self.sent = pieces
            plans = [from_columns([columns(q ^ j) for j in range(size)], part, len(widths)) for q in range(size)]
            out = rearrange(self.exchange_seq(pieces), [(part, w) for w in widths], plans, rank, F32)
            return [matrix.reshape(-1) for matrix in out]
        full = lax.all_gather(value, "seq", axis=0, tiled=False)
        plans = [from_columns([columns(b) for b in range(size)], rows, len(widths))]
        out = []
        for matrix in rearrange([full[b] for b in range(size)], [(rows, w) for w in widths], plans, dtype=F32):
            count = matrix.size // size
            out.append(lax.dynamic_slice_in_dim(matrix.reshape(-1), rank * count, count))
        return out


def in_columns(columns, rows):
    copies, place = [], 0
    for matrix, first, count in columns:
        copies.append((matrix, first, place, rows, count))
        place += count
    return copies


def from_columns(columns_of, rows, matrices):
    out = [[] for _ in range(matrices)]
    for which, columns in enumerate(columns_of):
        place = 0
        for matrix, first, count in columns:
            if matrix is not None:
                out[matrix].append((which, place, first, rows, count))
            place += count
    return out


def rearrange_kernel(plans, count, info, *refs):
    inputs, outputs = refs[:count], refs[count:]

    def run(plan):
        for out, copies in zip(outputs, plan):
            for which, first, place, rows, columns in copies:
                if which is None:
                    value = jnp.zeros((rows, columns), out.dtype)
                else:
                    value = inputs[which][:rows, first : first + columns].astype(out.dtype)
                out[:rows, place : place + columns] = value

    if len(plans) == 1:
        run(plans[0])
        return
    for rank, plan in enumerate(plans):
        pl.when(info[0] == rank)(partial(run, plan))


def rearrange(inputs, shapes, plans, rank=0, dtype=None):
    dtype = dtype or inputs[0].dtype
    spec = lambda shape: pl.BlockSpec(shape, lambda i, info: (0, 0))
    return pl.pallas_call(
        partial(rearrange_kernel, plans, len(inputs)),
        out_shape=[jax.ShapeDtypeStruct(shape, dtype) for shape in shapes],
        grid_spec=pltpu.PrefetchScalarGridSpec(
            num_scalar_prefetch=1,
            grid=(1,),
            in_specs=[spec(value.shape) for value in inputs],
            out_specs=[spec(shape) for shape in shapes],
        ),
        compiler_params=pltpu.CompilerParams(vmem_limit_bytes=40 << 20),
        cost_estimate=pl.CostEstimate(
            flops=0, transcendentals=0, bytes_accessed=2 * sum(value.size * value.dtype.itemsize for value in inputs)
        ),
        name="rearrange",
    )(jnp.asarray(rank, jnp.int32).reshape(1), *inputs)


class Ring:
    def __init__(self, size):
        self.size = size
        self.order = [*range(0, size, 2), *range(size - 1, 0, -2)] if size == 8 else list(range(size))
        self.groups = [self.order] if size == 8 else None

    def gather(self, value):
        return lax.all_gather(value, "dp", axis=0, tiled=True, axis_index_groups=self.groups)

    def scatter(self, value):
        total = lax.psum_scatter(value, "dp", scatter_dimension=0, tiled=True, axis_index_groups=self.groups)
        return lax.optimization_barrier(total)

    def inward(self, value, small=False):
        return self.blocks(value, self.order, small)

    def outward(self, value, small=False):
        return self.blocks(value, [self.order.index(d) for d in range(self.size)], small)

    def blocks(self, value, order, small):
        if self.groups is None:
            return value
        rows, width = value.shape
        part = width // self.size
        if small:
            plan = [(0, d * part, k * part, rows, part) for k, d in enumerate(order)]
            return rearrange([value], [value.shape], [[plan]])[0]
        return jnp.concatenate([value[:, d * part : (d + 1) * part] for d in order], axis=1)


def head_columns(index, size, width):
    own = -(-(width // HD) // size)
    even = own - own % 2

    def heads(part, first, count):
        start = min((index * own + first) * HD, width)
        stop = min(start + count * HD, width)
        out = [(0, part * width + start, stop - start), (None, 0, count * HD - stop + start)]
        return [entry for entry in out if entry[2]]

    out = [entry for part in range(3) for entry in heads(part, 0, even)]
    if own % 2:
        out += [entry for part in range(3) for entry in heads(part, even, 1)] + [(None, 0, HD)]
    return out


def hidden_columns(index, size, order, hidden):
    part = hidden // (len(order) * size)
    return [(0, (d * size + index) * part, part) for d in order]


def feature_columns(index, size, order, width, matrix):
    own, part = width // size, width // len(order)
    out, place = [], index * own
    while place < (index + 1) * own:
        stop = min((index + 1) * own, (place // part + 1) * part)
        out.append((matrix, order[place // part] * part + place % part, stop - place))
        place = stop
    return out


def half_masks():
    lane = lax.broadcasted_iota(jnp.int32, (1, LANES), 1)
    return [lane < HD, lane >= HD]


def row_block(ref, block, rows):
    return ref[pl.ds(pl.multiple_of(block * rows, rows), rows), :]


def attention_forward_kernel(size, pairs, odd, info, q_ref, k_ref, v_ref, o_ref, k_all, v_all):
    mine, length = info[0], info[1]
    count = q_ref.shape[0] // size
    pair = pl.program_id(0)
    last = pair == pairs - 1
    for a in range(size):
        rows = pl.ds(a * count, count)
        keys = row_block(k_ref, mine ^ a, count)
        if odd:
            keys = jnp.where(last, jnp.roll(keys, HD, axis=1), keys)
        k_all[rows, :] = keys
        v_all[rows, :] = row_block(v_ref, mine ^ a, count)
    halves = half_masks()
    zero = jnp.zeros((), BF)

    def one(a, half):
        span = (a + 1) * count
        q = jnp.where(half, row_block(q_ref, mine ^ a, count), zero)
        s = lax.dot_general(q, k_all[:span, :], (((1,), (1,)), ((), ())), preferred_element_type=F32) * 0.125
        limit = jnp.minimum(a * count + lax.broadcasted_iota(jnp.int32, (count, 1), 0), length - 1)
        allowed = lax.broadcasted_iota(jnp.int32, (count, span), 1) <= limit
        s = jnp.where(allowed, s, -1e30)
        e = jnp.exp(s - jnp.max(s, axis=1, keepdims=True))
        p = (e * (1.0 / jnp.sum(e, axis=1, keepdims=True))).astype(BF)
        return jnp.dot(p, v_all[:span, :], preferred_element_type=F32)

    for a in range(size):
        rows = pl.ds(pl.multiple_of((mine ^ a) * count, count), count)
        first = one(a, halves[0])
        if not odd:
            o_ref[rows, :] = jnp.where(halves[0], first, one(a, halves[1])).astype(BF)
            continue
        o_ref[rows, :] = jnp.where(halves[0], first, 0.0).astype(BF)

        @pl.when(jnp.logical_not(last))
        def _():
            o_ref[rows, :] = jnp.where(halves[0], o_ref[rows, :], one(a, halves[1]).astype(BF))


def attention_backward_kernel(size, pairs, odd, info, q_ref, k_ref, v_ref, g_ref, d_ref, k_all, v_all, dq, dk, dv):
    mine, length = info[0], info[1]
    count = q_ref.shape[0] // size
    pair = pl.program_id(0)
    last = pair == pairs - 1
    for a in range(size):
        rows = pl.ds(a * count, count)
        keys = row_block(k_ref, mine ^ a, count)
        if odd:
            keys = jnp.where(last, jnp.roll(keys, HD, axis=1), keys)
        k_all[rows, :] = keys
        v_all[rows, :] = row_block(v_ref, mine ^ a, count)
    dk[...] = jnp.zeros_like(dk)
    dv[...] = jnp.zeros_like(dv)
    halves = half_masks()
    zero = jnp.zeros((), BF)

    def one(a, which):
        half = halves[which]
        span = (a + 1) * count
        rows = pl.ds(a * count, count)
        q = jnp.where(half, row_block(q_ref, mine ^ a, count), zero)
        g = jnp.where(half, row_block(g_ref, mine ^ a, count), zero)
        keys, values = k_all[:span, :], v_all[:span, :]
        contract = (((1,), (1,)), ((), ()))
        s = lax.dot_general(keys, q, contract, preferred_element_type=F32) * 0.125
        limit = jnp.minimum(a * count + lax.broadcasted_iota(jnp.int32, (1, count), 1), length - 1)
        allowed = lax.broadcasted_iota(jnp.int32, (span, count), 0) <= limit
        s = jnp.where(allowed, s, -1e30)
        e = jnp.exp(s - jnp.max(s, axis=0, keepdims=True))
        p = e * (1.0 / jnp.sum(e, axis=0, keepdims=True))
        dp = lax.dot_general(values, g, contract, preferred_element_type=F32)
        inner = jnp.sum(p * dp, axis=0, keepdims=True)
        ds = (p * (dp - inner) * 0.125).astype(BF)
        dv[:span, :] += jnp.dot(p.astype(BF), g, preferred_element_type=F32)
        dk[:span, :] += jnp.dot(ds, q, preferred_element_type=F32)
        part = lax.dot_general(ds, keys, (((0,), (0,)), ((), ())), preferred_element_type=F32)
        if which == 0:
            dq[rows, :] = jnp.where(half, part, 0.0)
        else:
            dq[rows, :] = jnp.where(half, part, dq[rows, :])

    for a in range(size):
        one(a, 0)
    if odd:

        @pl.when(jnp.logical_not(last))
        def _():
            for a in range(size):
                one(a, 1)
    else:
        for a in range(size):
            one(a, 1)

    def store(block, value_of):
        cols = pl.ds(pl.multiple_of(block * LANES, LANES), LANES)
        for a in range(size):
            rows = pl.ds(pl.multiple_of((mine ^ a) * count, count), count)
            d_ref[rows, cols] = value_of(pl.ds(a * count, count)).astype(BF)

    full = pairs - 1 if odd else pairs

    def plain():
        store(pair, lambda r: dq[r, :])
        store(full + pair, lambda r: dk[r, :])
        store(2 * full + pair, lambda r: dv[r, :])

    if not odd:
        plain()
        return
    pl.when(jnp.logical_not(last))(plain)

    @pl.when(last)
    def _():
        store(3 * full, lambda r: jnp.where(halves[0], dq[r, :], jnp.roll(dk[r, :], HD, axis=1)))
        store(3 * full + 1, lambda r: jnp.where(halves[0], dv[r, :], 0.0))


def head_specs(span, pairs, odd):
    full = pairs - 1 if odd else pairs

    def spec(part):
        def index(j, info):
            if not odd:
                return (0, part * full + j)
            return (0, jnp.where(j < full, part * full + j, 3 * full + (part == 2)))

        return pl.BlockSpec((span, LANES), index)

    return [spec(0), spec(1), spec(2)]


def attention_forward(info, mixed, own, size):
    span = mixed.shape[0]
    pairs, odd = -(-own // 2), own % 2
    return pl.pallas_call(
        partial(attention_forward_kernel, size, pairs, odd),
        out_shape=jax.ShapeDtypeStruct((span, pairs * LANES), BF),
        grid_spec=pltpu.PrefetchScalarGridSpec(
            num_scalar_prefetch=1,
            grid=(pairs,),
            in_specs=head_specs(span, pairs, odd),
            out_specs=pl.BlockSpec((span, LANES), lambda j, info: (0, j)),
            scratch_shapes=[pltpu.VMEM((span, LANES), BF)] * 2,
        ),
        compiler_params=pltpu.CompilerParams(vmem_limit_bytes=40 << 20),
        cost_estimate=pl.CostEstimate(
            flops=own * span * span * 3400, transcendentals=0, bytes_accessed=mixed.size * 4
        ),
        name="attention_forward",
    )(info, mixed, mixed, mixed)


def attention_backward(info, mixed, grad, own, size):
    span = mixed.shape[0]
    pairs, odd = -(-own // 2), own % 2
    return pl.pallas_call(
        partial(attention_backward_kernel, size, pairs, odd),
        out_shape=jax.ShapeDtypeStruct(mixed.shape, BF),
        grid_spec=pltpu.PrefetchScalarGridSpec(
            num_scalar_prefetch=1,
            grid=(pairs,),
            in_specs=[*head_specs(span, pairs, odd), pl.BlockSpec((span, LANES), lambda j, info: (0, j))],
            out_specs=pl.BlockSpec(mixed.shape, lambda j, info: (0, 0)),
            scratch_shapes=[pltpu.VMEM((span, LANES), BF)] * 2 + [pltpu.VMEM((span, LANES), F32)] * 3,
        ),
        compiler_params=pltpu.CompilerParams(vmem_limit_bytes=48 << 20),
        cost_estimate=pl.CostEstimate(
            flops=own * span * span * 3400, transcendentals=0, bytes_accessed=mixed.size * 6
        ),
        name="attention_backward",
    )(info, mixed, mixed, mixed, grad)


def normal(value):
    centre = value - jnp.mean(value, axis=-1, keepdims=True)
    scale = lax.rsqrt(jnp.mean(centre * centre, axis=-1, keepdims=True) + EPS)
    return centre * scale, scale


def norm_input_grad(unit, scale, gain, grad):
    scaled = grad * gain
    return scale * (
        scaled
        - jnp.mean(scaled, axis=-1, keepdims=True)
        - unit * jnp.mean(scaled * unit, axis=-1, keepdims=True)
    )


ROOT = 0.7978845608028654
CUBIC = 0.044715


def gelu_and_slope(u):
    t = jnp.tanh(ROOT * (u + CUBIC * u * u * u))
    half = 0.5 * (1.0 + t)
    return u * half, half + 0.5 * u * (1.0 - t * t) * ROOT * (1.0 + 3.0 * CUBIC * u * u)


def dot(a, b, dims=((1,), (0,))):
    return lax.dot_general(a, b, (dims, ((), ())), preferred_element_type=F32)


def local(size, dps, tokens, cotangent, lengths, w_qkv, w_out, w_fc, w_proj, attention_vectors, block_vectors):
    _, count, width = tokens.shape
    heads = width // HD
    own = -(-heads // size)
    hidden = w_proj.shape[0] * dps * size // width
    rank = lax.axis_index("seq")
    row = lax.axis_index("dp")
    device = row * size + rank
    devices = dps * size
    length = lengths[0]
    info = jnp.stack([rank.astype(jnp.int32), length])
    unit_rows = width // dps

    links = Links(dps, size)

    ring = Ring(dps)
    quarter = width // size
    columns_qkv = lambda b: head_columns(b, size, width)
    columns_fc = lambda b: hidden_columns(b, size, ring.order, hidden)
    columns_attention = lambda b: columns_qkv(b) + feature_columns(b, size, ring.order, width, 1)

    def own_columns(value, columns):
        count = sum(entry[2] for entry in columns(0))
        plans = [[in_columns(columns(q), 1)] for q in range(size)]
        return rearrange([value.reshape(1, -1)], [(1, count)], plans, rank)[0][0]

    def all_columns(value, total, columns):
        plans = []
        for q in range(size):
            copies = from_columns([columns(q)], 1, 1)[0]
            for b in range(size):
                if b != q:
                    copies += [(None, 0, first, 1, count) for matrix, first, count in columns(b) if matrix is not None]
            plans.append([copies])
        return rearrange([value.reshape(1, -1)], [(1, total)], plans, rank)[0][0]

    split = lambda m: [m[j * count : (j + 1) * count] for j in range(size)]

    attention_part = links.columns_from_rows([w_qkv, w_out], unit_rows, columns_attention)
    attention_full = ring.gather(attention_part)
    qkv_full, out_part = attention_full[:, :-quarter], lax.optimization_barrier(attention_full[:, -quarter:])

    shift = hidden // devices
    tail = -(-shift * devices // LANES) * LANES
    before = links.shift(after(w_fc[-tail:], attention_part), 1)
    part = attention_vectors.shape[0]
    last = device == devices - 1
    small = jnp.zeros((8 * width,), BF)
    small = lax.dynamic_update_slice_in_dim(small, attention_vectors, device * part, 0)
    small = lax.dynamic_update_slice_in_dim(small, block_vectors, 4 * width + device * part, 0)
    small = jnp.concatenate([small, jnp.where(last, w_fc[-hidden:], jnp.zeros((), BF))])
    small = links.all_sum(after(small, attention_part), ("seq", "dp")).astype(F32)
    natural = small[: 8 * width].reshape(8, width)
    gain1, shift1, _, _, bias_o, gain2, shift2, bias_p = ring.inward(natural, small=True)
    bias_fc = own_columns(small[8 * width :], columns_fc)
    bias_qkv = own_columns(jnp.concatenate([natural[2], jnp.zeros_like(natural[2]), natural[3]]), columns_qkv)

    x_own = ring.inward(tokens[0])
    x_all = jnp.concatenate(links.gather_seq(after(x_own, attention_part)), axis=0)
    place = rank * count + jnp.arange(count)
    dy_own = ring.inward(cotangent[0]) * (place < length).astype(BF)[:, None]
    dy_wide = dy_own.astype(F32)
    dy = jnp.concatenate(links.gather_seq(after(dy_own, small, x_all)), axis=0)
    unit1_all, _ = normal(x_all.astype(F32))
    h1 = (unit1_all * gain1 + shift1).astype(BF)
    plain = w_fc.shape[0] - shift
    fc_flat = lax.dynamic_slice_in_dim(jnp.concatenate([before, after(w_fc, attention_part, dy, h1)]), tail - shift * device, plain)
    fc_part = links.columns_from_rows([fc_flat], unit_rows, columns_fc)
    fc_full = ring.gather(fc_part)

    out_parts = links.gather_seq(out_part, free=True)

    mixed = (dot(after(h1, dy), qkv_full) + bias_qkv).astype(BF)
    proj_full = ring.gather(after(ring.inward(w_proj.reshape(-1, width), small=True), fc_part, mixed))
    o_heads = attention_forward(info, mixed, own, size)
    out_parts = [after(piece, mixed) for piece in out_parts]
    o_got = links.relative(links.exchange_seq(split(o_heads)))
    o_own = jnp.concatenate([piece[:, : own * HD] for piece in o_got], axis=1)
    o_own = ring.inward(o_own[:, :width])
    projected = links.relative([dot(o_own, piece) for piece in out_parts])
    x2 = x_own.astype(F32) + jnp.concatenate(projected, axis=1) + bias_o
    unit2, scale2 = normal(x2)
    h2 = jnp.concatenate(links.gather_seq((unit2 * gain2 + shift2).astype(BF)), axis=0)

    u = dot(h2, fc_full) + bias_fc
    a, slope = gelu_and_slope(u)
    a, slope = a.astype(BF), slope.astype(BF)
    grad_proj = dot(a, dy, ((0,), (0,))).astype(BF)
    grad_proj_own = ring.scatter(grad_proj)
    du = (dot(after(dy, grad_proj), proj_full, ((1,), (1,))) * slope.astype(F32)).astype(BF)
    dh2_part = dot(du, fc_full, ((1,), (1,)))
    dh2 = links.scatter_seq(split(dh2_part))
    grad_fc = dot(h2, after(du, dh2_part), ((0,), (0,))).astype(BF)
    output_part = dot(after(a, grad_fc), proj_full)
    dh2 = after(dh2, output_part)
    grad_fc = ring.scatter(after(grad_fc, grad_proj_own))
    dx2 = dy_wide + norm_input_grad(unit2, scale2, gain2, dh2)
    dz = dx2.astype(BF)

    dz_parts = links.relative([dz[:, b * quarter : (b + 1) * quarter] for b in range(size)])
    do_own = sum(dot(dz_part, piece, ((1,), (1,))) for dz_part, piece in zip(dz_parts, out_parts))
    do_own = jnp.pad(ring.outward(do_own.astype(BF)), ((0, 0), (0, own * size * HD - width)))
    do_blocks = [jnp.pad(do_own[:, b * own * HD : (b + 1) * own * HD], ((0, 0), (0, own % 2 * HD))) for b in range(size)]
    do_blocks = links.relative(do_blocks)
    do_heads = jnp.concatenate(links.exchange_seq(do_blocks), axis=0)
    grad_out = [dot(after(o_own, *do_blocks), dz_part, ((0,), (0,))).astype(BF) for dz_part in dz_parts]
    do_heads = after(do_heads, *grad_out, grad_proj_own)
    dmixed = attention_backward(info, mixed, do_heads, own, size)
    grad_out = links.scatter_seq(grad_out, dmixed, free=True).astype(BF)
    dh1_part = dot(dmixed, qkv_full, ((1,), (1,)))
    grad_qkv = dot(h1, after(dmixed, dh1_part), ((0,), (0,))).astype(BF)
    grad_attention = jnp.concatenate([grad_qkv, grad_out], axis=1)
    dh1_part, dmixed, grad_fc = (after(value, grad_attention) for value in (dh1_part, dmixed, grad_fc))
    output = links.scatter_seq(split(output_part), free=True, hold=grad_attention)
    output = ring.outward((x2 + output + bias_p).astype(BF))
    grad_attention = ring.scatter(grad_attention)
    fc_rows = links.rows_from_columns(grad_fc, [hidden], columns_fc)[0]
    behind = links.shift(fc_rows[:tail].astype(BF), -1)
    total = lambda m: jnp.sum(m.astype(F32), axis=0)
    wide = all_columns(total(dmixed), 3 * width, columns_qkv)
    inner = [total(dh1_part * unit1_all), total(dh1_part), total(dz), total(dh2 * unit2), total(dh2), total(dy_wide)]
    grad_g1, grad_c1, grad_bo, grad_g2, grad_c2, grad_bp = ring.outward(jnp.stack(inner), small=True)
    sums = jnp.concatenate([
        grad_g1, grad_c1, wide[:width], wide[2 * width :], grad_bo, grad_g2, grad_c2, grad_bp,
        all_columns(total(after(du, grad_fc)), hidden, columns_fc),
    ])
    sums = links.all_sum(sums, ("seq",), free=True)
    dh1 = links.scatter_seq(split(dh1_part), free=True)
    qkv_flat, out_flat = links.rows_from_columns(grad_attention, [3 * width, width], columns_attention)
    dh1 = after(dh1, *links.sent)
    unit1, scale1 = normal(x_own.astype(F32))
    input_grad = ring.outward(dx2 + norm_input_grad(unit1, scale1, gain1, dh1))

    sums = links.all_sum(sums, ("dp",), free=True)
    vec1 = lax.dynamic_slice_in_dim(sums[: 4 * width], device * part, part)
    vec2 = lax.dynamic_slice_in_dim(sums[4 * width : 8 * width], device * part, part)
    sum_bf = sums[8 * width :]

    behind = jnp.where(last, jnp.pad(sum_bf, (0, tail - hidden)), behind.astype(F32))
    fc_flat_grad = lax.dynamic_slice_in_dim(
        jnp.concatenate([fc_rows, behind]), shift * device, w_fc.shape[0]
    )
    grad_attention = after(grad_attention, input_grad, fc_flat_grad, vec1, vec2, output)
    return (output[None], input_grad[None], qkv_flat, out_flat, fc_flat_grad, ring.outward(grad_proj_own, small=True).astype(F32).reshape(-1), vec1, vec2)


def solution(mesh):
    tokens = P("dp", "seq", None)
    flat = P(("dp", "seq"))
    return jax.shard_map(
        partial(local, mesh.shape["seq"], mesh.shape["dp"]),
        mesh=mesh,
        in_specs=(tokens, tokens, P("dp"), *[flat] * 6),
        out_specs=(tokens, tokens, *[flat] * 6),
        check_vma=False,
    )
```
